32 devices in a mesh: az: 4 (over z), rad: 2 (over x), ax: 4 (over y, core).
Axes of the slice: x: 2, y: 2, z: 4, core: 2. Of those that a mesh axis runs over, the one named last changes fastest.
Arguments:
- cycle: float32 [4, 5, 512, 4096], P(None, None, ('rad', 'ax'), 'az'), may hold values from -6 to 6
- field: float32 [5, 64, 8, 4096], P(None, 'rad', 'ax', 'az'), may hold values from -6 to 6
- shift: int32 [1], replicated, may hold values from 0 to 4095
- owner: int32 [64, 8], P('rad', 'ax'), may hold values 0 or 1
Outputs:
- field_next: float32 [5, 64, 8, 4096], P(None, 'rad', 'ax', 'az')
- shifted_cycle: float32 [4, 5, 512, 4096], P(None, None, ('rad', 'ax'), 'az')
The draws below stay inside these ranges and needn't reach their ends.
All inputs are finite; a program needn't handle non-finite values. No bound on the sum of `owner` on one device may be relied on, other than what follows from the above.
Results may differ from the reference program's by a relative error of at most 0.00007.
Values sent between devices are 32-bit elements; how exact they have to be, the bound alone decides.
A program may use at most 192 MiB of HBM per device.

```python
import math
import jax
import jax.numpy as jnp
from jax import lax

NTH = 4096
LAY = 4
VARS = 5
KR = 8
NR = 512
NRS = 64
NZS = 8


def plant(values, own_key, low, largest):
    spot = [jax.random.randint(jax.random.fold_in(own_key, axis), (), 0, length) for axis, length in enumerate(values.shape)]
    widest = values.shape.index(max(values.shape))
    next_to = spot[:widest] + [(spot[widest] + 1) % values.shape[widest]] + spot[widest + 1:]
    return values.at[tuple(spot)].set(low).at[tuple(next_to)].set(largest)


def block_levels(stream_key, shape, cuts, least, top_value):
    def one(dim, shards_of):
        draws = jax.random.uniform(jax.random.fold_in(jax.random.fold_in(stream_key, 6), dim), (shards_of,), jnp.float32, least / len(cuts), top_value / len(cuts))
        return jnp.repeat(jnp.exp(draws), shape[dim] // shards_of).reshape((-1,) + (1,) * (len(shape) - dim - 1))

    level = one(*cuts[0])
    for cut in cuts[1:]:
        level = level * one(*cut)
    return level


def centred(stream_key, extent, scale, bound, pieces=(), kind=jnp.bfloat16):
    drawn = scale * jax.random.normal(stream_key, extent, jnp.float32)
    if pieces:
        drawn = drawn * block_levels(stream_key, extent, pieces, -0.22, 0.18)
    return jnp.clip(drawn, -bound, bound).astype(kind)


def setup_inputs(seed: int = 0) -> dict:
    seeds = jax.random.split(jax.random.key(seed), 5)
    return {
        "cycle": centred(seeds[0], (LAY, VARS, NR, NTH), 1.0, 6.0, ((2, 8), (3, 4)), jnp.float32),
        "field": centred(seeds[1], (VARS, NRS, NZS, NTH), 1.0, 6.0, ((1, 2), (2, 4), (3, 4)), jnp.float32),
        "shift": jax.random.randint(seeds[2], (1,), 0, NTH).astype(jnp.int32),
        "owner": plant((jax.random.randint(seeds[3], (NRS, NZS), 0, 4) < 3).astype(jnp.int32), jax.random.fold_in(seeds[3], 1), 0, 1),
    }


LAYER_WEIGHTS = (0.4, 0.3, 0.2, 0.1)
AXIAL_SPEEDS = (0.35, 0.2, 0.3, 0.25, 0.4)
DIFFUSION = 0.15
SWIRL_SPEED = 0.1


def shift_layer(layer, shift):
    spectrum = jnp.fft.fft(layer, axis=-1)
    wave = jnp.arange(NTH, dtype=jnp.int32)
    folded = jnp.minimum(wave, NTH - wave)
    filt = (3 * folded < NTH).astype(jnp.float32)
    phase = jnp.remainder(wave * shift[0], NTH).astype(jnp.float32) * (2.0 * math.pi / NTH)
    gain = filt * jnp.exp(-1j * phase)
    return jnp.real(jnp.fft.ifft(spectrum * gain, axis=-1)).astype(jnp.float32)


def reference(cycle, field, shift, owner):
    shifted_cycle = lax.map(lambda layer: shift_layer(layer, shift), cycle)
    weights = jnp.array(LAYER_WEIGHTS, jnp.float32)
    grouped = shifted_cycle.reshape(LAY, VARS, NRS, KR, NTH)
    ghost = jnp.einsum('l,lvrkt->vrt', weights, grouped, precision=lax.Precision.HIGHEST) / KR
    mask = owner.astype(jnp.float32)[:, :, None]
    speeds = jnp.array(AXIAL_SPEEDS, jnp.float32)

    def advance(inputs):
        state0, ghost_var, speed = inputs

        def rates(state):
            radial_pad = jnp.pad(state, ((1, 1), (0, 0), (0, 0)))
            zeros_top = jnp.zeros_like(state[:, :1])
            axial_pad = jnp.concatenate([ghost_var[:, None], state, zeros_top], axis=1)
            outward = radial_pad[2:]
            inward = radial_pad[:-2]
            above = axial_pad[:, 2:]
            below = axial_pad[:, :-2]
            return mask * (DIFFUSION * (outward + inward + above + below - 4.0 * state)
                           - 0.5 * speed * (above - below) - 0.5 * SWIRL_SPEED * (outward - inward))

        first = rates(state0)
        second = rates(state0 + 0.5 * first)
        third = rates(state0 + 0.5 * second)
        fourth = rates(state0 + third)
        return state0 + (first + 2.0 * second + 2.0 * third + fourth) / 6.0

    field_next = lax.map(advance, (field, ghost, speeds))
    return field_next, shifted_cycle
```

```python
import math

import jax
import jax.numpy as jnp
import numpy as np
from jax import lax
from jax.experimental import pallas as pl
from jax.experimental.pallas import tpu as pltpu
from jax.sharding import PartitionSpec as P

KR = 8


LAYER_WEIGHTS = (0.4, 0.3, 0.2, 0.1)
AXIAL_SPEEDS = (0.35, 0.2, 0.3, 0.25, 0.4)
DIFFUSION = 0.15
SWIRL_SPEED = 0.1
MIB = 1024 * 1024


def class_counts(length):
    top = (length - 1) // 3
    kept = np.arange(-top, top + 1)
    first = kept[kept % 4 == 1]
    assert length % 4 == 0 and (first - 1).sum() == 0
    even, odd, half = [int((kept % 4 == r).sum()) for r in (0, 1, 2)]
    assert even == odd
    return even, half


def shift_tables(shift_value, length):
    quarter = length // 4
    even, half = class_counts(length)
    target = jnp.arange(quarter, dtype=jnp.int32) - shift_value
    rows = []
    for count in (even, half):
        angle = jnp.remainder(count * target, 2 * quarter).astype(jnp.float32) * (math.pi / quarter)
        rows += [jnp.sin(angle), jnp.cos(angle)]
    angle = jnp.remainder(target, length).astype(jnp.float32) * (2.0 * math.pi / length)
    rows += [jnp.cos(angle), jnp.sin(angle)]
    source = np.arange(quarter) * (2.0 * np.pi / length)
    rows += [jnp.asarray(np.cos(source), jnp.float32), jnp.asarray(np.sin(source), jnp.float32)]
    return jnp.stack(rows)


def source_tables(length):
    quarter = length // 4
    source = np.arange(quarter)
    cols = []
    for count in class_counts(length):
        angle = (count * source % (2 * quarter)) * (np.pi / quarter)
        cols += [np.sin(angle), np.cos(angle)]
    return jnp.asarray(np.stack(cols, axis=1), jnp.float32)


def matrix_values(length, first, block, shift_value, rows, cols):
    quarter = length // 4
    even, half = class_counts(length)
    shape = (block, quarter)
    source = lax.broadcasted_iota(jnp.int32, shape, 0) + first
    target = lax.broadcasted_iota(jnp.int32, shape, 1)
    apart = (target - source - shift_value) & (2 * quarter - 1)
    apart = jnp.where(apart >= quarter, apart - 2 * quarter, apart)
    near = jnp.where(apart > quarter // 2, quarter - apart, apart)
    near = jnp.where(apart < -(quarter // 2), -quarter - apart, near)
    u = near.astype(jnp.float32) * (math.pi / quarter)
    w = u * u
    poly = jnp.full(shape, 1.0 / 6227020800.0, jnp.float32)
    for c in (-1.0 / 39916800.0, 1.0 / 362880.0, -1.0 / 5040.0, 1.0 / 120.0, -1.0 / 6.0):
        poly = poly * w + c
    sine = u + u * (w * poly)
    zero = near == 0
    inverse = 0.25 / (quarter * jnp.where(zero, 1.0, sine))
    top_even = rows[0:1, :] * cols[:, 1:2] - rows[1:2, :] * cols[:, 0:1]
    top_half = rows[2:3, :] * cols[:, 3:4] - rows[3:4, :] * cols[:, 2:3]
    sign = jnp.where(apart == 0, 1.0, -1.0)
    m_even = jnp.where(zero, 0.25 * even / quarter, top_even * inverse)
    m_half = jnp.where(zero, sign * (0.25 * half / quarter), top_half * inverse)
    return split(m_even) + split(m_half)


def kernel_matrix_body(length, block, shift_ref, rows_ref, cols_ref, *out_refs):
    first = pl.program_id(0) * block
    values = matrix_values(length, first, block, shift_ref[0], rows_ref[...], cols_ref[...])
    for ref, value in zip(out_refs, values):
        ref[...] = value


def filter_matrices(shift, tables, length):
    quarter = length // 4
    block = 128
    out = jax.ShapeDtypeStruct((quarter, quarter), jnp.bfloat16)
    return pl.pallas_call(
        lambda *refs: kernel_matrix_body(length, block, *refs),
        grid=(quarter // block,),
        out_shape=[out] * 4,
        in_specs=[
            pl.BlockSpec(memory_space=pltpu.SMEM),
            pl.BlockSpec((8, quarter), lambda i: (0, 0)),
            pl.BlockSpec((block, 4), lambda i: (i, 0)),
        ],
        out_specs=[pl.BlockSpec((block, quarter), lambda i: (i, 0))] * 4,
        compiler_params=pltpu.CompilerParams(vmem_limit_bytes=32 * MIB),
        cost_estimate=pl.CostEstimate(flops=60 * quarter * quarter, bytes_accessed=8 * quarter * quarter, transcendentals=0),
        name="filter_matrices",
    )(shift, tables, source_tables(length))


def split(value):
    high = value.astype(jnp.bfloat16)
    return high, (value - high.astype(jnp.float32)).astype(jnp.bfloat16)


def product(value, high_ref, low_ref):
    high, low = split(value)
    f32 = jnp.float32
    return (
        jnp.dot(high, low_ref[...], preferred_element_type=f32)
        + jnp.dot(low, high_ref[...], preferred_element_type=f32)
        + jnp.dot(high, high_ref[...], preferred_element_type=f32)
    )


def filter_quarters(parts, tab_ref, matrix_refs):
    x0, x1, x2, x3 = parts
    count = x0.shape[0]
    eh_ref, el_ref, hh_ref, hl_ref = matrix_refs
    cos_t, sin_t = 2.0 * tab_ref[4:5, :], 2.0 * tab_ref[5:6, :]
    cos_s, sin_s = tab_ref[6:7, :], tab_ref[7:8, :]
    even, odd = x0 + x2, x1 + x3
    re, im = x0 - x2, x3 - x1
    stacked = jnp.concatenate([even + odd, re * cos_s + im * sin_s, im * cos_s - re * sin_s], axis=0)
    turned = product(stacked, eh_ref, el_ref)
    z2 = product(even - odd, hh_ref, hl_ref)
    z0, ure, uim = turned[:count], turned[count : 2 * count], turned[2 * count :]
    zre = cos_t * ure - sin_t * uim
    zim = cos_t * uim + sin_t * ure
    plus, minus = z0 + z2, z0 - z2
    return plus + zre, minus - zim, plus - zre, minus + zim


def filter_body(x_ref, tab_ref, eh_ref, el_ref, hh_ref, hl_ref, out_ref):
    values = filter_quarters([x_ref[i] for i in range(4)], tab_ref, (eh_ref, el_ref, hh_ref, hl_ref))
    for i, value in enumerate(values):
        out_ref[i] = value


def filtered(quarters, tables, matrices):
    _, count, quarter = quarters.shape
    block = next((b for b in (80, 64, 40, 32, 16, 8) if count % b == 0), count)
    whole = pl.BlockSpec((quarter, quarter), lambda i: (0, 0))
    part = pl.BlockSpec((4, block, quarter), lambda i: (0, i, 0))
    return pl.pallas_call(
        filter_body,
        grid=(count // block,),
        out_shape=jax.ShapeDtypeStruct(quarters.shape, jnp.float32),
        in_specs=[part, pl.BlockSpec((8, quarter), lambda i: (0, 0))] + [whole] * 4,
        out_specs=part,
        compiler_params=pltpu.CompilerParams(vmem_limit_bytes=48 * MIB),
        cost_estimate=pl.CostEstimate(
            flops=24 * count * quarter * quarter,
            bytes_accessed=32 * count * quarter + 8 * quarter * quarter,
            transcendentals=0,
        ),
        name="spectral_filter",
    )(quarters, tables, *matrices)


def to_quarters(pieces):
    sectors, count, sector = pieces.shape
    per = sectors // 4
    if per == 1:
        return pieces
    return pieces.reshape(4, per, count, sector).transpose(0, 2, 1, 3).reshape(4, count, per * sector)


def to_sectors(quarters, sectors):
    _, count, quarter = quarters.shape
    per = sectors // 4
    if per == 1:
        return quarters
    sector = quarter // per
    return quarters.reshape(4, count, per, sector).transpose(0, 2, 1, 3).reshape(sectors, count, sector)


def still_tables(length):
    quarter = length // 4
    target = np.arange(quarter)
    rows = []
    for count in class_counts(length):
        angle = (count * target % (2 * quarter)) * (np.pi / quarter)
        rows += [np.sin(angle), np.cos(angle)]
    angle = target * (2.0 * np.pi / length)
    rows += [np.cos(angle), np.sin(angle)] * 2
    return jnp.asarray(np.stack(rows), jnp.float32)


def turn_values(shift_value, length):
    quarter = length // 4
    even, half = class_counts(length)
    steps = jnp.array([2 * even, 2 * half, 1], jnp.int32) * shift_value
    angle = jnp.remainder(steps, length).astype(jnp.float32) * (2.0 * math.pi / length)
    return jnp.concatenate([jnp.sin(angle), jnp.cos(angle)])


def step_body(length, turn_ref, shift_ref, owner_ref, rows_ref, cols_ref, cycle_ref, field_ref, out_ref, next_ref,
              land, done, eh, el, hh, hl, tab, loaded, state, under, over, ghost, ghost_out, change,
              send_sem, recv_sem, back_send, back_recv, own_sem, store_sem, load_sem,
              ghost_send, ghost_recv, axial_send, axial_recv, radial_send, radial_recv):
    layers, variables, radial, sector = cycle_ref.shape
    quarter = length // 4
    block = radial // 4
    owned = block // KR
    cells = radial // KR
    height = next_ref.shape[1]
    az, rad, ax = lax.axis_index("az"), lax.axis_index("rad"), lax.axis_index("ax")
    rads, axes = lax.axis_size("rad"), lax.axis_size("ax")
    inner, outer = rad > 0, rad < rads - 1
    inlet, lower, upper = ax == 0, ax > 0, ax < axes - 1
    matrices = (eh, el, hh, hl)
    mesh_id = pl.DeviceIdType.MESH

    @pl.when(jnp.logical_not(upper))
    def _():
        over[...] = jnp.zeros_like(over)

    @pl.when(jnp.logical_not(inner))
    def _():
        state[:, :, :, 0] = jnp.zeros((4, 2, variables, 8, 128), jnp.float32)

    @pl.when(jnp.logical_not(outer))
    def _():
        state[:, :, :, height + 1] = jnp.zeros((4, 2, variables, 8, 128), jnp.float32)

    barrier = pltpu.get_barrier_semaphore()
    for i in range(4):
        for j in range(axes):
            if i + j > 0:
                peer = {"az": lax.rem(az + i, 4), "ax": lax.rem(ax + j, axes)}
                pl.semaphore_signal(barrier, inc=1, device_id=peer, device_id_type=mesh_id)

    @pl.when(inner)
    def _():
        pl.semaphore_signal(barrier, inc=1, device_id={"rad": rad - 1}, device_id_type=mesh_id)

    @pl.when(outer)
    def _():
        pl.semaphore_signal(barrier, inc=1, device_id={"rad": rad + 1}, device_id_type=mesh_id)

    pl.semaphore_wait(barrier, 4 * axes - 1 + inner.astype(jnp.int32) + outer.astype(jnp.int32))

    def partner(k):
        return (None, az + 1 - 2 * lax.rem(az, 2), lax.rem(az + 2, 4), 3 - az)[k]

    def rows_of(index):
        return pl.ds(pl.multiple_of(index * block, block), block)

    def remote(src, dst, send, recv, peer):
        return pltpu.make_async_remote_copy(
            src_ref=src, dst_ref=dst, send_sem=send, recv_sem=recv, device_id=peer, device_id_type=mesh_id
        )

    def forth(v, k):
        peer = partner(k)
        return remote(
            cycle_ref.at[:, v, rows_of(peer)], land.at[v, az], send_sem.at[v, k - 1], recv_sem.at[v, k - 1], {"az": peer}
        )

    def back(v, k):
        peer = partner(k)
        return remote(
            done.at[v, peer], out_ref.at[:, v, rows_of(az)], back_send.at[v, k - 1], back_recv.at[v, k - 1], {"az": peer}
        )

    def own(v):
        return pltpu.make_async_copy(cycle_ref.at[:, v, rows_of(az)], land.at[v, az], own_sem.at[v])

    def store(v):
        return pltpu.make_async_copy(done.at[v, az], out_ref.at[:, v, rows_of(az)], store_sem.at[v])

    def ghost_copy(v, i, source, first):
        to = lax.rem(az + i, 4)
        return remote(
            ghost_out.at[v, to], ghost.at[v, pl.ds(first, owned)], ghost_send.at[v, i], ghost_recv.at[v, source], {"az": to, "ax": 0}
        )

    def ghost_to(v, i):
        return ghost_copy(v, i, 4 * ax + az, ax * cells + az * owned)

    def ghost_from(v, i, j):
        source = lax.rem(az + i, 4)
        return ghost_copy(v, i, 4 * j + source, j * cells + source * owned)

    def raise_copy(s):
        return remote(state.at[s, 1, :, pl.ds(1, height)], under.at[s], axial_send.at[s, 0], axial_recv.at[s, 0], {"ax": ax + 1})

    def lower_copy(s):
        return remote(state.at[s, 0, :, pl.ds(1, height)], over.at[s], axial_send.at[s, 1], axial_recv.at[s, 1], {"ax": ax - 1})

    def outward_copy(s):
        return remote(state.at[s, :, :, height], state.at[s, :, :, 0], radial_send.at[s, 0], radial_recv.at[s, 0], {"rad": rad + 1})

    def inward_copy(s):
        return remote(state.at[s, :, :, 1], state.at[s, :, :, height + 1], radial_send.at[s, 1], radial_recv.at[s, 1], {"rad": rad - 1})

    def send_halo(s):
        for there, copy in ((upper, raise_copy), (lower, lower_copy), (outer, outward_copy), (inner, inward_copy)):
            @pl.when(there)
            def _():
                copy(s).start()

    def receive_halo(s):
        for there, copy in ((lower, raise_copy), (upper, lower_copy), (inner, outward_copy), (outer, inward_copy)):
            @pl.when(there)
            def _():
                copy(s).wait_recv()

    def halo_sent(s):
        for there, copy in ((upper, raise_copy), (lower, lower_copy), (outer, outward_copy), (inner, inward_copy)):
            @pl.when(there)
            def _():
                copy(s).wait_send()

    def start_forth(v, carry):
        for k in (2, 3, 1):
            forth(v, k).start()
        own(v).start()
        return carry

    load = pltpu.make_async_copy(field_ref, loaded, load_sem.at[0])
    load.start()
    lax.fori_loop(0, variables, start_forth, 0)
    load.wait()

    def unweave(r, carry):
        for v in range(variables):
            for z in range(2):
                state[0, z, v, r + 1] = loaded[v, r, pl.ds(z, 8, stride=2), :]
        return carry

    lax.fori_loop(0, height, unweave, 0)
    send_halo(0)

    tab[...] = rows_ref[...]
    for at, turn in ((0, 0), (2, 1)):
        sine, cosine = rows_ref[at : at + 1, :], rows_ref[at + 1 : at + 2, :]
        tab[at : at + 1, :] = sine * turn_ref[3 + turn] - cosine * turn_ref[turn]
        tab[at + 1 : at + 2, :] = cosine * turn_ref[3 + turn] + sine * turn_ref[turn]
    cosine, sine = rows_ref[4:5, :], rows_ref[5:6, :]
    tab[4:5, :] = cosine * turn_ref[5] + sine * turn_ref[2]
    tab[5:6, :] = sine * turn_ref[5] - cosine * turn_ref[2]

    def build(i, carry):
        first = pl.multiple_of(i * 128, 128)
        rows = pl.ds(first, 128)
        values = matrix_values(length, first, 128, shift_ref[0], tab[...], cols_ref[rows, :])
        for ref, value in zip(matrices, values):
            ref[rows, :] = value
        return carry

    lax.fori_loop(0, quarter // 128, build, 0)

    def chunk(v, carry):
        own(v).wait()
        for k in (2, 3, 1):
            forth(v, k).wait_recv()
        parts = [land[v, i].reshape(layers * block, sector) for i in range(4)]
        for i, value in enumerate(filter_quarters(parts, tab, matrices)):
            value = value.reshape(layers, block, sector)
            done[v, i] = value
            total = LAYER_WEIGHTS[0] * value[0]
            for layer in range(1, layers):
                total = total + LAYER_WEIGHTS[layer] * value[layer]
            mean = jnp.sum(total.reshape(owned, KR, sector), axis=1) / KR
            for cell in range(owned):
                for tile in range(8):
                    ghost_out[v, i, cell, tile : tile + 1, :] = mean[cell : cell + 1, tile * 128 : (tile + 1) * 128]
        for k in (2, 3, 1):
            back(v, k).start()
        store(v).start()

        @pl.when(inlet)
        def _():
            ghost[v, pl.ds(az * owned, owned)] = ghost_out[v, az]

        @pl.when(lower)
        def _():
            ghost_to(v, 0).start()

        for i in (1, 2, 3):
            ghost_to(v, i).start()
        return carry

    lax.fori_loop(0, variables, chunk, 0)

    @pl.when(inlet)
    def _():
        def arrive(v, carry):
            for j in range(axes):
                for i in range(4):
                    if i + j > 0:
                        ghost_from(v, i, j).wait_recv()
            return carry

        lax.fori_loop(0, variables, arrive, 0)

    for s in range(4):
        receive_halo(s)

        def advance(r, carry):
            for v in range(variables):
                here = [state[s, z, v, r + 1] for z in range(2)]
                below = [jnp.where(inlet, ghost[v, r], under[s, v, r]), here[0]]
                above = [here[1], over[s, v, r]]
                for z in range(2):
                    inward, outward = state[s, z, v, r], state[s, z, v, r + 2]
                    mask = owner_ref[r, z].astype(jnp.float32)
                    rate = mask * (
                        DIFFUSION * (outward + inward + above[z] + below[z] - 4.0 * here[z])
                        - (0.5 * AXIAL_SPEEDS[v]) * (above[z] - below[z])
                        - (0.5 * SWIRL_SPEED) * (outward - inward)
                    )
                    if s == 0:
                        change[z, v, r] = rate
                    elif s < 3:
                        change[z, v, r] = change[z, v, r] + 2.0 * rate
                    start = here[z] if s == 0 else state[0, z, v, r + 1]
                    if s < 3:
                        state[s + 1, z, v, r + 1] = start + (0.5, 0.5, 1.0)[s] * rate
                    else:
                        next_ref[v, r, pl.ds(z, 8, stride=2), :] = start + (change[z, v, r] + rate) / 6.0
            return carry

        lax.fori_loop(0, height, advance, 0)
        if s < 3:
            send_halo(s + 1)

    def finish(v, carry):
        for k in (2, 3, 1):
            forth(v, k).wait_send()
            back(v, k).wait_send()
            back(v, k).wait_recv()
        store(v).wait()

        @pl.when(lower)
        def _():
            ghost_to(v, 0).wait_send()

        for i in (1, 2, 3):
            ghost_to(v, i).wait_send()
        return carry

    lax.fori_loop(0, variables, finish, 0)
    for s in range(4):
        halo_sent(s)


def whole_step(cycle, field, shift, owner):
    layers, variables, radial, sector = cycle.shape
    _, height, _, _ = field.shape
    length = 4 * sector
    axes = lax.axis_size("ax")
    block = radial // 4
    owned = block // KR
    f32, bf16 = jnp.float32, jnp.bfloat16
    smem = pl.BlockSpec(memory_space=pltpu.SMEM)
    vmem = pl.BlockSpec(memory_space=pltpu.VMEM)
    hbm = pl.BlockSpec(memory_space=pl.ANY)
    dma = pltpu.SemaphoreType.DMA
    woven = (variables, height, 16, 128)
    plane = (variables, height, 8, 128)
    shifted_cycle, stepped = pl.pallas_call(
        lambda *refs: step_body(length, *refs),
        out_shape=[jax.ShapeDtypeStruct(cycle.shape, f32), jax.ShapeDtypeStruct(woven, f32)],
        in_specs=[smem, smem, smem, vmem, vmem, hbm, hbm],
        out_specs=[hbm, vmem],
        scratch_shapes=[pltpu.VMEM((variables, 4, layers, block, sector), f32)] * 2
        + [pltpu.VMEM((sector, sector), bf16)] * 4
        + [
            pltpu.VMEM((8, sector), f32),
            pltpu.VMEM(woven, f32),
            pltpu.VMEM((4, 2, variables, height + 2, 8, 128), f32),
            pltpu.VMEM((4,) + plane, f32),
            pltpu.VMEM((4,) + plane, f32),
            pltpu.VMEM(plane, f32),
            pltpu.VMEM((variables, 4, owned, 8, 128), f32),
            pltpu.VMEM((2,) + plane, f32),
        ]
        + [dma((variables, 3))] * 4
        + [dma((variables,))] * 2
        + [dma((1,)), dma((variables, 4)), dma((variables, 4 * axes))]
        + [dma((4, 2))] * 4,
        compiler_params=pltpu.CompilerParams(vmem_limit_bytes=54 * MIB, collective_id=0, has_side_effects=True),
        cost_estimate=pl.CostEstimate(
            flops=24 * layers * variables * radial * sector * sector,
            bytes_accessed=8 * layers * variables * radial * sector,
            transcendentals=0,
        ),
        name="whole_step",
    )(
        turn_values(shift[0], length),
        shift,
        owner,
        still_tables(length),
        source_tables(length),
        cycle,
        field.reshape(variables, height, 2, 8, 128).transpose(0, 1, 3, 2, 4).reshape(woven),
    )
    field_next = stepped.reshape(variables, height, 8, 2, 128).transpose(0, 1, 3, 2, 4).reshape(field.shape)
    return field_next, shifted_cycle


def shifted(array, axis, dim, width):
    devices, length = (lax.axis_size(axis), array.shape[dim])
    up = [(i, (i + 1) % devices) for i in range(devices - 1)]
    down = [(j, i) for i, j in up]
    last = lax.slice_in_dim(array, length - width, length, axis=dim)
    leading = lax.slice_in_dim(array, 0, width, axis=dim)
    return lax.ppermute(last, axis, up), lax.ppermute(leading, axis, down)


def chunked(cycle, shift):
    layers, variables, radial, sector = cycle.shape
    sectors = lax.axis_size("az")
    length = sectors * sector
    shift_value = shift[0]
    tables = shift_tables(shift_value, length)
    matrices = filter_matrices(shift, tables, length)

    def across(part):
        return lax.all_to_all(part, "az", split_axis=0, concat_axis=0, tiled=True)

    def passed(pieces):
        return to_sectors(filtered(to_quarters(pieces), tables, matrices), sectors)

    lead = cycle[:1].reshape(sectors, -1, sector)
    rest = cycle[1:].reshape(sectors, -1, sector)
    lead = across(lead)

    weights = jnp.array(LAYER_WEIGHTS, jnp.float32)
    cells = radial // KR
    grouped = cycle.reshape(layers, variables, cells, KR, sector)
    mean = jnp.sum(jnp.sum(grouped * weights[:, None, None, None, None], axis=0), axis=2) / KR
    around = lax.all_gather(mean.reshape(variables * cells, sector), "az", axis=0, tiled=False)
    lead, around, rest = lax.optimization_barrier((lead, around, rest))
    rest = across(rest)

    ghost = lax.dynamic_index_in_dim(passed(around), lax.axis_index("az"), 0, keepdims=False)

    lead, rest = lax.optimization_barrier((passed(lead), rest))
    lead = across(lead).reshape(1, variables, radial, sector)
    rest = across(passed(rest)).reshape(layers - 1, variables, radial, sector)
    shifted_cycle = jnp.concatenate([lead, rest], axis=0)
    return ghost, shifted_cycle


def on_device(cycle, field, shift, owner):
    layers, variables, radial, sector = cycle.shape
    sectors = lax.axis_size("az")
    if sectors == 4 and sector == 1024 and field.shape[2] == 2 and radial % (4 * KR) == 0:
        return whole_step(cycle, field, shift, owner)
    ghost, shifted_cycle = chunked(cycle, shift)
    ghost = lax.all_gather(ghost.reshape(variables, radial // KR, sector), "ax", axis=1, tiled=True)

    mask = owner.astype(jnp.float32)[None, :, :, None]
    speeds = jnp.array(AXIAL_SPEEDS, jnp.float32)[:, None, None, None]
    at_inlet = lax.axis_index("ax") == 0

    def rates(state):
        inner, outer = shifted(state, "rad", 1, 1)
        under, over = shifted(state, "ax", 2, 1)
        lower = jnp.where(at_inlet, ghost[:, :, None], under)
        outward = jnp.concatenate([state[:, 1:], outer], axis=1)
        inward = jnp.concatenate([inner, state[:, :-1]], axis=1)
        above = jnp.concatenate([state[:, :, 1:], over], axis=2)
        below = jnp.concatenate([lower, state[:, :, :-1]], axis=2)
        return mask * (
            DIFFUSION * (outward + inward + above + below - 4.0 * state)
            - 0.5 * speeds * (above - below)
            - 0.5 * SWIRL_SPEED * (outward - inward)
        )

    first = rates(field)
    second = rates(field + 0.5 * first)
    third = rates(field + 0.5 * second)
    fourth = rates(field + third)
    field_next = field + (first + 2.0 * second + 2.0 * third + fourth) / 6.0
    return (field_next, shifted_cycle)


def solution(mesh):
    in_specs = (P(None, None, ("rad", "ax"), "az"), P(None, "rad", "ax", "az"), P(), P("rad", "ax"))
    out_specs = (P(None, "rad", "ax", "az"), P(None, None, ("rad", "ax"), "az"))
    return jax.shard_map(
        on_device, mesh=mesh, in_specs=in_specs, out_specs=out_specs, check_vma=False
    )
```

```python
import math

import jax
import jax.numpy as jnp
import numpy as np
from jax import lax
from jax.experimental import pallas as pl
from jax.experimental.pallas import tpu as pltpu
from jax.sharding import PartitionSpec as P

KR = 8


LAYER_WEIGHTS = (0.4, 0.3, 0.2, 0.1)
AXIAL_SPEEDS = (0.35, 0.2, 0.3, 0.25, 0.4)
DIFFUSION = 0.15
SWIRL_SPEED = 0.1
MIB = 1024 * 1024


def class_counts(length):
    top = (length - 1) // 3
    kept = np.arange(-top, top + 1)
    first = kept[kept % 4 == 1]
    assert length % 4 == 0 and (first - 1).sum() == 0
    even, odd, half = [int((kept % 4 == r).sum()) for r in (0, 1, 2)]
    assert even == odd
    return even, half


def shift_tables(shift_value, length):
    quarter = length // 4
    even, half = class_counts(length)
    target = jnp.arange(quarter, dtype=jnp.int32) - shift_value
    rows = []
    for count in (even, half):
        angle = jnp.remainder(count * target, 2 * quarter).astype(jnp.float32) * (math.pi / quarter)
        rows += [jnp.sin(angle), jnp.cos(angle)]
    angle = jnp.remainder(target, length).astype(jnp.float32) * (2.0 * math.pi / length)
    rows += [jnp.cos(angle), jnp.sin(angle)]
    source = np.arange(quarter) * (2.0 * np.pi / length)
    rows += [jnp.asarray(np.cos(source), jnp.float32), jnp.asarray(np.sin(source), jnp.float32)]
    return jnp.stack(rows)


def source_tables(length):
    quarter = length // 4
    source = np.arange(quarter)
    cols = []
    for count in class_counts(length):
        angle = (count * source % (2 * quarter)) * (np.pi / quarter)
        cols += [np.sin(angle), np.cos(angle)]
    return jnp.asarray(np.stack(cols, axis=1), jnp.float32)


def matrix_values(length, first, block, shift_value, rows, cols):
    quarter = length // 4
    even, half = class_counts(length)
    shape = (block, quarter)
    source = lax.broadcasted_iota(jnp.int32, shape, 0) + first
    target = lax.broadcasted_iota(jnp.int32, shape, 1)
    apart = (target - source - shift_value) & (2 * quarter - 1)
    apart = jnp.where(apart >= quarter, apart - 2 * quarter, apart)
    near = jnp.where(apart > quarter // 2, quarter - apart, apart)
    near = jnp.where(apart < -(quarter // 2), -quarter - apart, near)
    u = near.astype(jnp.float32) * (math.pi / quarter)
    w = u * u
    poly = jnp.full(shape, 1.0 / 6227020800.0, jnp.float32)
    for c in (-1.0 / 39916800.0, 1.0 / 362880.0, -1.0 / 5040.0, 1.0 / 120.0, -1.0 / 6.0):
        poly = poly * w + c
    sine = u + u * (w * poly)
    zero = near == 0
    inverse = 0.25 / (quarter * jnp.where(zero, 1.0, sine))
    top_even = rows[0:1, :] * cols[:, 1:2] - rows[1:2, :] * cols[:, 0:1]
    top_half = rows[2:3, :] * cols[:, 3:4] - rows[3:4, :] * cols[:, 2:3]
    sign = jnp.where(apart == 0, 1.0, -1.0)
    m_even = jnp.where(zero, 0.25 * even / quarter, top_even * inverse)
    m_half = jnp.where(zero, sign * (0.25 * half / quarter), top_half * inverse)
    return split(m_even) + split(m_half)


def kernel_matrix_body(length, block, shift_ref, rows_ref, cols_ref, *out_refs):
    first = pl.program_id(0) * block
    values = matrix_values(length, first, block, shift_ref[0], rows_ref[...], cols_ref[...])
    for ref, value in zip(out_refs, values):
        ref[...] = value


def filter_matrices(shift, tables, length):
    quarter = length // 4
    block = 128
    out = jax.ShapeDtypeStruct((quarter, quarter), jnp.bfloat16)
    return pl.pallas_call(
        lambda *refs: kernel_matrix_body(length, block, *refs),
        grid=(quarter // block,),
        out_shape=[out] * 4,
        in_specs=[
            pl.BlockSpec(memory_space=pltpu.SMEM),
            pl.BlockSpec((8, quarter), lambda i: (0, 0)),
            pl.BlockSpec((block, 4), lambda i: (i, 0)),
        ],
        out_specs=[pl.BlockSpec((block, quarter), lambda i: (i, 0))] * 4,
        compiler_params=pltpu.CompilerParams(vmem_limit_bytes=32 * MIB),
        cost_estimate=pl.CostEstimate(flops=60 * quarter * quarter, bytes_accessed=8 * quarter * quarter, transcendentals=0),
        name="filter_matrices",
    )(shift, tables, source_tables(length))


def split(value):
    high = value.astype(jnp.bfloat16)
    return high, (value - high.astype(jnp.float32)).astype(jnp.bfloat16)


def product(value, high_ref, low_ref):
    high, low = split(value)
    f32 = jnp.float32
    return (
        jnp.dot(high, low_ref[...], preferred_element_type=f32)
        + jnp.dot(low, high_ref[...], preferred_element_type=f32)
        + jnp.dot(high, high_ref[...], preferred_element_type=f32)
    )


def filter_quarters(parts, tab_ref, matrix_refs):
    x0, x1, x2, x3 = parts
    count = x0.shape[0]
    eh_ref, el_ref, hh_ref, hl_ref = matrix_refs
    cos_t, sin_t = 2.0 * tab_ref[4:5, :], 2.0 * tab_ref[5:6, :]
    cos_s, sin_s = tab_ref[6:7, :], tab_ref[7:8, :]
    even, odd = x0 + x2, x1 + x3
    re, im = x0 - x2, x3 - x1
    stacked = jnp.concatenate([even + odd, re * cos_s + im * sin_s, im * cos_s - re * sin_s], axis=0)
    turned = product(stacked, eh_ref, el_ref)
    z2 = product(even - odd, hh_ref, hl_ref)
    z0, ure, uim = turned[:count], turned[count : 2 * count], turned[2 * count :]
    zre = cos_t * ure - sin_t * uim
    zim = cos_t * uim + sin_t * ure
    plus, minus = z0 + z2, z0 - z2
    return plus + zre, minus - zim, plus - zre, minus + zim


def filter_body(x_ref, tab_ref, eh_ref, el_ref, hh_ref, hl_ref, out_ref):
    values = filter_quarters([x_ref[i] for i in range(4)], tab_ref, (eh_ref, el_ref, hh_ref, hl_ref))
    for i, value in enumerate(values):
        out_ref[i] = value


def filtered(quarters, tables, matrices):
    _, count, quarter = quarters.shape
    block = next((b for b in (80, 64, 40, 32, 16, 8) if count % b == 0), count)
    whole = pl.BlockSpec((quarter, quarter), lambda i: (0, 0))
    part = pl.BlockSpec((4, block, quarter), lambda i: (0, i, 0))
    return pl.pallas_call(
        filter_body,
        grid=(count // block,),
        out_shape=jax.ShapeDtypeStruct(quarters.shape, jnp.float32),
        in_specs=[part, pl.BlockSpec((8, quarter), lambda i: (0, 0))] + [whole] * 4,
        out_specs=part,
        compiler_params=pltpu.CompilerParams(vmem_limit_bytes=48 * MIB),
        cost_estimate=pl.CostEstimate(
            flops=24 * count * quarter * quarter,
            bytes_accessed=32 * count * quarter + 8 * quarter * quarter,
            transcendentals=0,
        ),
        name="spectral_filter",
    )(quarters, tables, *matrices)


def to_quarters(pieces):
    sectors, count, sector = pieces.shape
    per = sectors // 4
    if per == 1:
        return pieces
    return pieces.reshape(4, per, count, sector).transpose(0, 2, 1, 3).reshape(4, count, per * sector)


def to_sectors(quarters, sectors):
    _, count, quarter = quarters.shape
    per = sectors // 4
    if per == 1:
        return quarters
    sector = quarter // per
    return quarters.reshape(4, count, per, sector).transpose(0, 2, 1, 3).reshape(sectors, count, sector)


def still_tables(length):
    quarter = length // 4
    target = np.arange(quarter)
    rows = []
    for count in class_counts(length):
        angle = (count * target % (2 * quarter)) * (np.pi / quarter)
        rows += [np.sin(angle), np.cos(angle)]
    angle = target * (2.0 * np.pi / length)
    rows += [np.cos(angle), np.sin(angle)] * 2
    return jnp.asarray(np.stack(rows), jnp.float32)


def turn_values(shift_value, length):
    quarter = length // 4
    even, half = class_counts(length)
    steps = jnp.array([2 * even, 2 * half, 1], jnp.int32) * shift_value
    angle = jnp.remainder(steps, length).astype(jnp.float32) * (2.0 * math.pi / length)
    return jnp.concatenate([jnp.sin(angle), jnp.cos(angle)])


def step_body(length, turn_ref, shift_ref, owner_ref, rows_ref, cols_ref, cycle_ref, field_ref, out_ref, next_ref,
              land, done, eh, el, hh, hl, tab, loaded, state, under, over, ghost, ghost_in, ghost_out, change,
              send_sem, recv_sem, back_send, back_recv, own_sem, store_sem, load_sem,
              ghost_send, ghost_recv, inlet_recv, axial_send, axial_recv, radial_send, radial_recv):
    layers, variables, radial, sector = cycle_ref.shape
    quarter = length // 4
    block = radial // 4
    owned = block // KR
    cells = radial // KR
    height = next_ref.shape[1]
    az, rad, ax = lax.axis_index("az"), lax.axis_index("rad"), lax.axis_index("ax")
    rads, axes = lax.axis_size("rad"), lax.axis_size("ax")
    inner, outer = rad > 0, rad < rads - 1
    inlet, lower, upper = ax == 0, ax > 0, ax < axes - 1
    matrices = (eh, el, hh, hl)
    mesh_id = pl.DeviceIdType.MESH

    @pl.when(jnp.logical_not(upper))
    def _():
        over[...] = jnp.zeros_like(over)

    @pl.when(jnp.logical_not(inner))
    def _():
        state[:, :, :, 0] = jnp.zeros((4, 2, variables, 8, 128), jnp.float32)

    @pl.when(jnp.logical_not(outer))
    def _():
        state[:, :, :, height + 1] = jnp.zeros((4, 2, variables, 8, 128), jnp.float32)

    barrier = pltpu.get_barrier_semaphore()
    for peer in [{"az": lax.rem(az + i, 4)} for i in (1, 2, 3)] + [{"ax": lax.rem(ax + j, axes)} for j in range(1, axes)]:
        pl.semaphore_signal(barrier, inc=1, device_id=peer, device_id_type=mesh_id)

    @pl.when(inner)
    def _():
        pl.semaphore_signal(barrier, inc=1, device_id={"rad": rad - 1}, device_id_type=mesh_id)

    @pl.when(outer)
    def _():
        pl.semaphore_signal(barrier, inc=1, device_id={"rad": rad + 1}, device_id_type=mesh_id)

    pl.semaphore_wait(barrier, axes + 2 + inner.astype(jnp.int32) + outer.astype(jnp.int32))

    def partner(k):
        return (None, az + 1 - 2 * lax.rem(az, 2), lax.rem(az + 2, 4), 3 - az)[k]

    def rows_of(index):
        return pl.ds(pl.multiple_of(index * block, block), block)

    def remote(src, dst, send, recv, peer):
        return pltpu.make_async_remote_copy(
            src_ref=src, dst_ref=dst, send_sem=send, recv_sem=recv, device_id=peer, device_id_type=mesh_id
        )

    def forth(v, k):
        peer = partner(k)
        return remote(
            cycle_ref.at[:, v, rows_of(peer)], land.at[v, az], send_sem.at[v, k - 1], recv_sem.at[v, k - 1], {"az": peer}
        )

    def back(v, k):
        peer = partner(k)
        return remote(
            done.at[v, peer], out_ref.at[:, v, rows_of(az)], back_send.at[v, k - 1], back_recv.at[v, k - 1], {"az": peer}
        )

    def own(v):
        return pltpu.make_async_copy(cycle_ref.at[:, v, rows_of(az)], land.at[v, az], own_sem.at[v])

    def store(v):
        return pltpu.make_async_copy(done.at[v, az], out_ref.at[:, v, rows_of(az)], store_sem.at[v])

    def ghost_back(v, k):
        peer = partner(k)
        return remote(
            ghost_out.at[v, peer], ghost_in.at[v, pl.ds(az * owned, owned)],
            ghost_send.at[v, k], ghost_recv.at[v, k], {"az": peer},
        )

    def ghost_down(v, source):
        return remote(
            ghost_in.at[v], ghost.at[v, pl.ds(source * cells, cells)],
            ghost_send.at[v, 0], inlet_recv.at[v, source], {"ax": 0},
        )

    def raise_copy(s):
        return remote(state.at[s, 1, :, pl.ds(1, height)], under.at[s], axial_send.at[s, 0], axial_recv.at[s, 0], {"ax": ax + 1})

    def lower_copy(s):
        return remote(state.at[s, 0, :, pl.ds(1, height)], over.at[s], axial_send.at[s, 1], axial_recv.at[s, 1], {"ax": ax - 1})

    def outward_copy(s):
        return remote(state.at[s, :, :, height], state.at[s, :, :, 0], radial_send.at[s, 0], radial_recv.at[s, 0], {"rad": rad + 1})

    def inward_copy(s):
        return remote(state.at[s, :, :, 1], state.at[s, :, :, height + 1], radial_send.at[s, 1], radial_recv.at[s, 1], {"rad": rad - 1})

    def send_halo(s):
        for there, copy in ((upper, raise_copy), (lower, lower_copy), (outer, outward_copy), (inner, inward_copy)):
            @pl.when(there)
            def _():
                copy(s).start()

    def receive_halo(s):
        for there, copy in ((lower, raise_copy), (upper, lower_copy), (inner, outward_copy), (outer, inward_copy)):
            @pl.when(there)
            def _():
                copy(s).wait_recv()

    def halo_sent(s):
        for there, copy in ((upper, raise_copy), (lower, lower_copy), (outer, outward_copy), (inner, inward_copy)):
            @pl.when(there)
            def _():
                copy(s).wait_send()

    def start_forth(v, carry):
        for k in (2, 3, 1):
            forth(v, k).start()
        own(v).start()
        return carry

    def start_back(v, carry):
        for k in (2, 3, 1):
            back(v, k).start()
        return carry

    load = pltpu.make_async_copy(field_ref, loaded, load_sem.at[0])
    load.start()
    lax.fori_loop(0, variables, start_forth, 0)
    load.wait()

    def unweave(r, carry):
        for v in range(variables):
            for z in range(2):
                state[0, z, v, r + 1] = loaded[v, r, pl.ds(z, 8, stride=2), :]
        return carry

    lax.fori_loop(0, height, unweave, 0)
    send_halo(0)

    tab[...] = rows_ref[...]
    for at, turn in ((0, 0), (2, 1)):
        sine, cosine = rows_ref[at : at + 1, :], rows_ref[at + 1 : at + 2, :]
        tab[at : at + 1, :] = sine * turn_ref[3 + turn] - cosine * turn_ref[turn]
        tab[at + 1 : at + 2, :] = cosine * turn_ref[3 + turn] + sine * turn_ref[turn]
    cosine, sine = rows_ref[4:5, :], rows_ref[5:6, :]
    tab[4:5, :] = cosine * turn_ref[5] + sine * turn_ref[2]
    tab[5:6, :] = sine * turn_ref[5] - cosine * turn_ref[2]

    def build(i, carry):
        first = pl.multiple_of(i * 128, 128)
        rows = pl.ds(first, 128)
        values = matrix_values(length, first, 128, shift_ref[0], tab[...], cols_ref[rows, :])
        for ref, value in zip(matrices, values):
            ref[rows, :] = value
        return carry

    lax.fori_loop(0, quarter // 128, build, 0)

    def chunk(v, carry):
        own(v).wait()
        for k in (2, 3, 1):
            forth(v, k).wait_recv()
        parts = [land[v, i].reshape(layers * block, sector) for i in range(4)]
        for i, value in enumerate(filter_quarters(parts, tab, matrices)):
            value = value.reshape(layers, block, sector)
            done[v, i] = value
            total = LAYER_WEIGHTS[0] * value[0]
            for layer in range(1, layers):
                total = total + LAYER_WEIGHTS[layer] * value[layer]
            mean = jnp.sum(total.reshape(owned, KR, sector), axis=1) / KR
            for cell in range(owned):
                for tile in range(8):
                    ghost_out[v, i, cell, tile : tile + 1, :] = mean[cell : cell + 1, tile * 128 : (tile + 1) * 128]
        store(v).start()
        ghost_in[v, pl.ds(az * owned, owned)] = ghost_out[v, az]
        for k in (2, 3, 1):
            ghost_back(v, k).start()

        @pl.when(v == variables - 2)
        def _():
            start_back(0, 0)

        return carry

    lax.fori_loop(0, variables, chunk, 0)
    lax.fori_loop(1, variables, start_back, 0)

    def collect(v, carry):
        for k in (2, 3, 1):
            ghost_back(v, k).wait_recv()

        @pl.when(inlet)
        def _():
            ghost[v, pl.ds(0, cells)] = ghost_in[v]

        @pl.when(lower)
        def _():
            ghost_down(v, ax).start()

        return carry

    lax.fori_loop(0, variables, collect, 0)

    @pl.when(inlet)
    def _():
        def arrive(v, carry):
            for source in range(1, axes):
                ghost_down(v, source).wait_recv()
            return carry

        lax.fori_loop(0, variables, arrive, 0)

    for s in range(4):
        receive_halo(s)

        def advance(r, carry):
            for v in range(variables):
                here = [state[s, z, v, r + 1] for z in range(2)]
                below = [jnp.where(inlet, ghost[v, r], under[s, v, r]), here[0]]
                above = [here[1], over[s, v, r]]
                for z in range(2):
                    inward, outward = state[s, z, v, r], state[s, z, v, r + 2]
                    mask = owner_ref[r, z].astype(jnp.float32)
                    rate = mask * (
                        DIFFUSION * (outward + inward + above[z] + below[z] - 4.0 * here[z])
                        - (0.5 * AXIAL_SPEEDS[v]) * (above[z] - below[z])
                        - (0.5 * SWIRL_SPEED) * (outward - inward)
                    )
                    if s == 0:
                        change[z, v, r] = rate
                    elif s < 3:
                        change[z, v, r] = change[z, v, r] + 2.0 * rate
                    start = here[z] if s == 0 else state[0, z, v, r + 1]
                    if s < 3:
                        state[s + 1, z, v, r + 1] = start + (0.5, 0.5, 1.0)[s] * rate
                    else:
                        next_ref[v, r, pl.ds(z, 8, stride=2), :] = start + (change[z, v, r] + rate) / 6.0
            return carry

        lax.fori_loop(0, height, advance, 0)
        if s < 3:
            send_halo(s + 1)

    def finish(v, carry):
        for k in (2, 3, 1):
            forth(v, k).wait_send()
            back(v, k).wait_send()
            back(v, k).wait_recv()
            ghost_back(v, k).wait_send()
        store(v).wait()

        @pl.when(lower)
        def _():
            ghost_down(v, ax).wait_send()

        return carry

    lax.fori_loop(0, variables, finish, 0)
    for s in range(4):
        halo_sent(s)


def whole_step(cycle, field, shift, owner):
    layers, variables, radial, sector = cycle.shape
    _, height, _, _ = field.shape
    length = 4 * sector
    axes = lax.axis_size("ax")
    block = radial // 4
    owned = block // KR
    f32, bf16 = jnp.float32, jnp.bfloat16
    smem = pl.BlockSpec(memory_space=pltpu.SMEM)
    vmem = pl.BlockSpec(memory_space=pltpu.VMEM)
    hbm = pl.BlockSpec(memory_space=pl.ANY)
    dma = pltpu.SemaphoreType.DMA
    woven = (variables, height, 16, 128)
    plane = (variables, height, 8, 128)
    shifted_cycle, stepped = pl.pallas_call(
        lambda *refs: step_body(length, *refs),
        out_shape=[jax.ShapeDtypeStruct(cycle.shape, f32), jax.ShapeDtypeStruct(woven, f32)],
        in_specs=[smem, smem, smem, vmem, vmem, hbm, hbm],
        out_specs=[hbm, vmem],
        scratch_shapes=[pltpu.VMEM((variables, 4, layers, block, sector), f32)] * 2
        + [pltpu.VMEM((sector, sector), bf16)] * 4
        + [
            pltpu.VMEM((8, sector), f32),
            pltpu.VMEM(woven, f32),
            pltpu.VMEM((4, 2, variables, height + 2, 8, 128), f32),
            pltpu.VMEM((4,) + plane, f32),
            pltpu.VMEM((4,) + plane, f32),
            pltpu.VMEM(plane, f32),
            pltpu.VMEM((variables, 4 * owned, 8, 128), f32),
            pltpu.VMEM((variables, 4, owned, 8, 128), f32),
            pltpu.VMEM((2,) + plane, f32),
        ]
        + [dma((variables, 3))] * 4
        + [dma((variables,))] * 2
        + [dma((1,)), dma((variables, 4)), dma((variables, 4)), dma((variables, axes))]
        + [dma((4, 2))] * 4,
        compiler_params=pltpu.CompilerParams(vmem_limit_bytes=54 * MIB, collective_id=0, has_side_effects=True),
        cost_estimate=pl.CostEstimate(
            flops=24 * layers * variables * radial * sector * sector,
            bytes_accessed=8 * layers * variables * radial * sector,
            transcendentals=0,
        ),
        name="whole_step",
    )(
        turn_values(shift[0], length),
        shift,
        owner,
        still_tables(length),
        source_tables(length),
        cycle,
        field.reshape(variables, height, 2, 8, 128).transpose(0, 1, 3, 2, 4).reshape(woven),
    )
    field_next = stepped.reshape(variables, height, 8, 2, 128).transpose(0, 1, 3, 2, 4).reshape(field.shape)
    return field_next, shifted_cycle


def shifted(array, axis, dim, width):
    devices, length = (lax.axis_size(axis), array.shape[dim])
    up = [(i, (i + 1) % devices) for i in range(devices - 1)]
    down = [(j, i) for i, j in up]
    last = lax.slice_in_dim(array, length - width, length, axis=dim)
    leading = lax.slice_in_dim(array, 0, width, axis=dim)
    return lax.ppermute(last, axis, up), lax.ppermute(leading, axis, down)


def chunked(cycle, shift):
    layers, variables, radial, sector = cycle.shape
    sectors = lax.axis_size("az")
    length = sectors * sector
    shift_value = shift[0]
    tables = shift_tables(shift_value, length)
    matrices = filter_matrices(shift, tables, length)

    def across(part):
        return lax.all_to_all(part, "az", split_axis=0, concat_axis=0, tiled=True)

    def passed(pieces):
        return to_sectors(filtered(to_quarters(pieces), tables, matrices), sectors)

    lead = cycle[:1].reshape(sectors, -1, sector)
    rest = cycle[1:].reshape(sectors, -1, sector)
    lead = across(lead)

    weights = jnp.array(LAYER_WEIGHTS, jnp.float32)
    cells = radial // KR
    grouped = cycle.reshape(layers, variables, cells, KR, sector)
    mean = jnp.sum(jnp.sum(grouped * weights[:, None, None, None, None], axis=0), axis=2) / KR
    around = lax.all_gather(mean.reshape(variables * cells, sector), "az", axis=0, tiled=False)
    lead, around, rest = lax.optimization_barrier((lead, around, rest))
    rest = across(rest)

    ghost = lax.dynamic_index_in_dim(passed(around), lax.axis_index("az"), 0, keepdims=False)

    lead, rest = lax.optimization_barrier((passed(lead), rest))
    lead = across(lead).reshape(1, variables, radial, sector)
    rest = across(passed(rest)).reshape(layers - 1, variables, radial, sector)
    shifted_cycle = jnp.concatenate([lead, rest], axis=0)
    return ghost, shifted_cycle


def on_device(cycle, field, shift, owner):
    layers, variables, radial, sector = cycle.shape
    sectors = lax.axis_size("az")
    if sectors == 4 and sector == 1024 and field.shape[2] == 2 and radial % (4 * KR) == 0:
        return whole_step(cycle, field, shift, owner)
    ghost, shifted_cycle = chunked(cycle, shift)
    ghost = lax.all_gather(ghost.reshape(variables, radial // KR, sector), "ax", axis=1, tiled=True)

    mask = owner.astype(jnp.float32)[None, :, :, None]
    speeds = jnp.array(AXIAL_SPEEDS, jnp.float32)[:, None, None, None]
    at_inlet = lax.axis_index("ax") == 0

    def rates(state):
        inner, outer = shifted(state, "rad", 1, 1)
        under, over = shifted(state, "ax", 2, 1)
        lower = jnp.where(at_inlet, ghost[:, :, None], under)
        outward = jnp.concatenate([state[:, 1:], outer], axis=1)
        inward = jnp.concatenate([inner, state[:, :-1]], axis=1)
        above = jnp.concatenate([state[:, :, 1:], over], axis=2)
        below = jnp.concatenate([lower, state[:, :, :-1]], axis=2)
        return mask * (
            DIFFUSION * (outward + inward + above + below - 4.0 * state)
            - 0.5 * speeds * (above - below)
            - 0.5 * SWIRL_SPEED * (outward - inward)
        )

    first = rates(field)
    second = rates(field + 0.5 * first)
    third = rates(field + 0.5 * second)
    fourth = rates(field + third)
    field_next = field + (first + 2.0 * second + 2.0 * third + fourth) / 6.0
    return (field_next, shifted_cycle)


def solution(mesh):
    in_specs = (P(None, None, ("rad", "ax"), "az"), P(None, "rad", "ax", "az"), P(), P("rad", "ax"))
    out_specs = (P(None, "rad", "ax", "az"), P(None, None, ("rad", "ax"), "az"))
    return jax.shard_map(
        on_device, mesh=mesh, in_specs=in_specs, out_specs=out_specs, check_vma=False
    )
```

```python
import math

import jax
import jax.numpy as jnp
import numpy as np
from jax import lax
from jax.experimental import pallas as pl
from jax.experimental.pallas import tpu as pltpu
from jax.sharding import PartitionSpec as P

KR = 8


LAYER_WEIGHTS = (0.4, 0.3, 0.2, 0.1)
AXIAL_SPEEDS = (0.35, 0.2, 0.3, 0.25, 0.4)
DIFFUSION = 0.15
SWIRL_SPEED = 0.1
MIB = 1024 * 1024


def class_counts(length):
    top = (length - 1) // 3
    kept = np.arange(-top, top + 1)
    first = kept[kept % 4 == 1]
    assert length % 4 == 0 and (first - 1).sum() == 0
    even, odd, half = [int((kept % 4 == r).sum()) for r in (0, 1, 2)]
    assert even == odd
    return even, half


def shift_tables(shift_value, length):
    quarter = length // 4
    even, half = class_counts(length)
    target = jnp.arange(quarter, dtype=jnp.int32) - shift_value
    rows = []
    for count in (even, half):
        angle = jnp.remainder(count * target, 2 * quarter).astype(jnp.float32) * (math.pi / quarter)
        rows += [jnp.sin(angle), jnp.cos(angle)]
    angle = jnp.remainder(target, length).astype(jnp.float32) * (2.0 * math.pi / length)
    rows += [jnp.cos(angle), jnp.sin(angle)]
    source = np.arange(quarter) * (2.0 * np.pi / length)
    rows += [jnp.asarray(np.cos(source), jnp.float32), jnp.asarray(np.sin(source), jnp.float32)]
    return jnp.stack(rows)


def source_tables(length):
    quarter = length // 4
    source = np.arange(quarter)
    cols = []
    for count in class_counts(length):
        angle = (count * source % (2 * quarter)) * (np.pi / quarter)
        cols += [np.sin(angle), np.cos(angle)]
    return jnp.asarray(np.stack(cols, axis=1), jnp.float32)


def matrix_values(length, first, block, shift_value, rows, cols):
    quarter = length // 4
    even, half = class_counts(length)
    shape = (block, quarter)
    source = lax.broadcasted_iota(jnp.int32, shape, 0) + first
    target = lax.broadcasted_iota(jnp.int32, shape, 1)
    apart = (target - source - shift_value) & (2 * quarter - 1)
    apart = jnp.where(apart >= quarter, apart - 2 * quarter, apart)
    near = jnp.where(apart > quarter // 2, quarter - apart, apart)
    near = jnp.where(apart < -(quarter // 2), -quarter - apart, near)
    u = near.astype(jnp.float32) * (math.pi / quarter)
    w = u * u
    poly = jnp.full(shape, 1.0 / 6227020800.0, jnp.float32)
    for c in (-1.0 / 39916800.0, 1.0 / 362880.0, -1.0 / 5040.0, 1.0 / 120.0, -1.0 / 6.0):
        poly = poly * w + c
    sine = u + u * (w * poly)
    zero = near == 0
    inverse = 0.25 / (quarter * jnp.where(zero, 1.0, sine))
    top_even = rows[0:1, :] * cols[:, 1:2] - rows[1:2, :] * cols[:, 0:1]
    top_half = rows[2:3, :] * cols[:, 3:4] - rows[3:4, :] * cols[:, 2:3]
    sign = jnp.where(apart == 0, 1.0, -1.0)
    m_even = jnp.where(zero, 0.25 * even / quarter, top_even * inverse)
    m_half = jnp.where(zero, sign * (0.25 * half / quarter), top_half * inverse)
    return split(m_even) + split(m_half)


def kernel_matrix_body(length, block, shift_ref, rows_ref, cols_ref, *out_refs):
    first = pl.program_id(0) * block
    values = matrix_values(length, first, block, shift_ref[0], rows_ref[...], cols_ref[...])
    for ref, value in zip(out_refs, values):
        ref[...] = value


def filter_matrices(shift, tables, length):
    quarter = length // 4
    block = 128
    out = jax.ShapeDtypeStruct((quarter, quarter), jnp.bfloat16)
    return pl.pallas_call(
        lambda *refs: kernel_matrix_body(length, block, *refs),
        grid=(quarter // block,),
        out_shape=[out] * 4,
        in_specs=[
            pl.BlockSpec(memory_space=pltpu.SMEM),
            pl.BlockSpec((8, quarter), lambda i: (0, 0)),
            pl.BlockSpec((block, 4), lambda i: (i, 0)),
        ],
        out_specs=[pl.BlockSpec((block, quarter), lambda i: (i, 0))] * 4,
        compiler_params=pltpu.CompilerParams(vmem_limit_bytes=32 * MIB),
        cost_estimate=pl.CostEstimate(flops=60 * quarter * quarter, bytes_accessed=8 * quarter * quarter, transcendentals=0),
        name="filter_matrices",
    )(shift, tables, source_tables(length))


def split(value):
    high = value.astype(jnp.bfloat16)
    return high, (value - high.astype(jnp.float32)).astype(jnp.bfloat16)


def product(value, high_ref, low_ref):
    high, low = split(value)
    f32 = jnp.float32
    return (
        jnp.dot(high, low_ref[...], preferred_element_type=f32)
        + jnp.dot(low, high_ref[...], preferred_element_type=f32)
        + jnp.dot(high, high_ref[...], preferred_element_type=f32)
    )


def filter_quarters(parts, tab_ref, matrix_refs):
    x0, x1, x2, x3 = parts
    count = x0.shape[0]
    eh_ref, el_ref, hh_ref, hl_ref = matrix_refs
    cos_t, sin_t = 2.0 * tab_ref[4:5, :], 2.0 * tab_ref[5:6, :]
    cos_s, sin_s = tab_ref[6:7, :], tab_ref[7:8, :]
    even, odd = x0 + x2, x1 + x3
    re, im = x0 - x2, x3 - x1
    stacked = jnp.concatenate([even + odd, re * cos_s + im * sin_s, im * cos_s - re * sin_s], axis=0)
    turned = product(stacked, eh_ref, el_ref)
    z2 = product(even - odd, hh_ref, hl_ref)
    z0, ure, uim = turned[:count], turned[count : 2 * count], turned[2 * count :]
    zre = cos_t * ure - sin_t * uim
    zim = cos_t * uim + sin_t * ure
    plus, minus = z0 + z2, z0 - z2
    return plus + zre, minus - zim, plus - zre, minus + zim


def filter_body(x_ref, tab_ref, eh_ref, el_ref, hh_ref, hl_ref, out_ref):
    values = filter_quarters([x_ref[i] for i in range(4)], tab_ref, (eh_ref, el_ref, hh_ref, hl_ref))
    for i, value in enumerate(values):
        out_ref[i] = value


def filtered(quarters, tables, matrices):
    _, count, quarter = quarters.shape
    block = next((b for b in (80, 64, 40, 32, 16, 8) if count % b == 0), count)
    whole = pl.BlockSpec((quarter, quarter), lambda i: (0, 0))
    part = pl.BlockSpec((4, block, quarter), lambda i: (0, i, 0))
    return pl.pallas_call(
        filter_body,
        grid=(count // block,),
        out_shape=jax.ShapeDtypeStruct(quarters.shape, jnp.float32),
        in_specs=[part, pl.BlockSpec((8, quarter), lambda i: (0, 0))] + [whole] * 4,
        out_specs=part,
        compiler_params=pltpu.CompilerParams(vmem_limit_bytes=48 * MIB),
        cost_estimate=pl.CostEstimate(
            flops=24 * count * quarter * quarter,
            bytes_accessed=32 * count * quarter + 8 * quarter * quarter,
            transcendentals=0,
        ),
        name="spectral_filter",
    )(quarters, tables, *matrices)


def to_quarters(pieces):
    sectors, count, sector = pieces.shape
    per = sectors // 4
    if per == 1:
        return pieces
    return pieces.reshape(4, per, count, sector).transpose(0, 2, 1, 3).reshape(4, count, per * sector)


def to_sectors(quarters, sectors):
    _, count, quarter = quarters.shape
    per = sectors // 4
    if per == 1:
        return quarters
    sector = quarter // per
    return quarters.reshape(4, count, per, sector).transpose(0, 2, 1, 3).reshape(sectors, count, sector)


def step_body(length, shift_ref, owner_ref, cycle_ref, field_ref, out_ref, next_ref,
              land, done, eh, el, hh, hl, tab, loaded, state, under, over, ghost, ghost_in, ghost_out, change,
              send_sem, recv_sem, back_send, back_recv, own_sem, store_sem, load_sem,
              ghost_send, ghost_recv, inlet_recv, axial_send, axial_recv, radial_send, radial_recv):
    layers, variables, radial, sector = cycle_ref.shape
    quarter = length // 4
    block = radial // 4
    owned = block // KR
    cells = radial // KR
    height = next_ref.shape[1]
    az, rad, ax = lax.axis_index("az"), lax.axis_index("rad"), lax.axis_index("ax")
    rads, axes = lax.axis_size("rad"), lax.axis_size("ax")
    inner, outer = rad > 0, rad < rads - 1
    inlet, lower, upper = ax == 0, ax > 0, ax < axes - 1
    matrices = (eh, el, hh, hl)
    mesh_id = pl.DeviceIdType.MESH

    barrier = pltpu.get_barrier_semaphore()
    for peer in [{"az": lax.rem(az + i, 4)} for i in (1, 2, 3)] + [{"ax": lax.rem(ax + j, axes)} for j in range(1, axes)]:
        pl.semaphore_signal(barrier, inc=1, device_id=peer, device_id_type=mesh_id)

    @pl.when(inner)
    def _():
        pl.semaphore_signal(barrier, inc=1, device_id={"rad": rad - 1}, device_id_type=mesh_id)

    @pl.when(outer)
    def _():
        pl.semaphore_signal(barrier, inc=1, device_id={"rad": rad + 1}, device_id_type=mesh_id)

    pl.semaphore_wait(barrier, axes + 2 + inner.astype(jnp.int32) + outer.astype(jnp.int32))

    def partner(k):
        return (None, az + 1 - 2 * lax.rem(az, 2), lax.rem(az + 2, 4), 3 - az)[k]

    def rows_of(index):
        return pl.ds(pl.multiple_of(index * block, block), block)

    def remote(src, dst, send, recv, peer):
        return pltpu.make_async_remote_copy(
            src_ref=src, dst_ref=dst, send_sem=send, recv_sem=recv, device_id=peer, device_id_type=mesh_id
        )

    def forth(v, k):
        peer = partner(k)
        return remote(
            cycle_ref.at[:, v, rows_of(peer)], land.at[v, az], send_sem.at[v, k - 1], recv_sem.at[v, k - 1], {"az": peer}
        )

    def back(v, k):
        peer = partner(k)
        return remote(
            done.at[v, peer], out_ref.at[:, v, rows_of(az)], back_send.at[v, k - 1], back_recv.at[v, k - 1], {"az": peer}
        )

    def own(v):
        return pltpu.make_async_copy(cycle_ref.at[:, v, rows_of(az)], land.at[v, az], own_sem.at[v])

    def store(v):
        return pltpu.make_async_copy(done.at[v, az], out_ref.at[:, v, rows_of(az)], store_sem.at[v])

    def ghost_back(v, k):
        peer = partner(k)
        return remote(
            ghost_out.at[v, peer], ghost_in.at[v, pl.ds(az * owned, owned)],
            ghost_send.at[v, k], ghost_recv.at[v, k], {"az": peer},
        )

    def ghost_down(v, source):
        return remote(
            ghost_in.at[v], ghost.at[v, pl.ds(source * cells, cells)],
            ghost_send.at[v, 0], inlet_recv.at[v, source], {"ax": 0},
        )

    def raise_copy(s):
        return remote(state.at[s, 1, :, pl.ds(1, height)], under.at[s], axial_send.at[s, 0], axial_recv.at[s, 0], {"ax": ax + 1})

    def lower_copy(s):
        return remote(state.at[s, 0, :, pl.ds(1, height)], over.at[s], axial_send.at[s, 1], axial_recv.at[s, 1], {"ax": ax - 1})

    def outward_copy(s):
        return remote(state.at[s, :, :, height], state.at[s, :, :, 0], radial_send.at[s, 0], radial_recv.at[s, 0], {"rad": rad + 1})

    def inward_copy(s):
        return remote(state.at[s, :, :, 1], state.at[s, :, :, height + 1], radial_send.at[s, 1], radial_recv.at[s, 1], {"rad": rad - 1})

    def send_halo(s):
        for there, copy in ((upper, raise_copy), (lower, lower_copy), (outer, outward_copy), (inner, inward_copy)):
            @pl.when(there)
            def _():
                copy(s).start()

    def receive_halo(s):
        for there, copy in ((lower, raise_copy), (upper, lower_copy), (inner, outward_copy), (outer, inward_copy)):
            @pl.when(there)
            def _():
                copy(s).wait_recv()

    def halo_sent(s):
        for there, copy in ((upper, raise_copy), (lower, lower_copy), (outer, outward_copy), (inner, inward_copy)):
            @pl.when(there)
            def _():
                copy(s).wait_send()

    def start_forth(v, carry):
        for k in (2, 3, 1):
            forth(v, k).start()
        own(v).start()
        return carry

    def start_back(v, carry):
        for k in (2, 3, 1):
            back(v, k).start()
        return carry

    load = pltpu.make_async_copy(field_ref, loaded, load_sem.at[0])
    load.start()
    lax.fori_loop(0, variables, start_forth, 0)
    load.wait()

    @pl.when(jnp.logical_not(upper))
    def _():
        over[...] = jnp.zeros_like(over)

    @pl.when(jnp.logical_not(inner))
    def _():
        state[:, :, :, 0] = jnp.zeros((4, 2, variables, 8, 128), jnp.float32)

    @pl.when(jnp.logical_not(outer))
    def _():
        state[:, :, :, height + 1] = jnp.zeros((4, 2, variables, 8, 128), jnp.float32)

    def unweave(r, carry):
        for v in range(variables):
            for z in range(2):
                state[0, z, v, r + 1] = loaded[v, r, pl.ds(z, 8, stride=2), :]
        return carry

    lax.fori_loop(0, height, unweave, 0)
    send_halo(0)

    even, half = class_counts(length)
    row = lax.broadcasted_iota(jnp.int32, (8, quarter), 0)
    target = lax.broadcasted_iota(jnp.int32, (8, quarter), 1)
    count = jnp.where(row < 2, 2 * even, jnp.where(row < 4, 2 * half, 1))
    angle = (count * (target - jnp.where(row < 6, shift_ref[0], 0))) & (length - 1)
    angle = angle.astype(jnp.float32) * (2.0 * math.pi / length)
    sines = (row == 0) | (row == 2) | (row == 5) | (row == 7)
    tab[...] = jnp.where(sines, jnp.sin(angle), jnp.cos(angle))

    def build(i, carry):
        first = pl.multiple_of(i * 128, 128)
        rows = pl.ds(first, 128)
        source = lax.broadcasted_iota(jnp.int32, (128, 4), 0) + first
        column = lax.broadcasted_iota(jnp.int32, (128, 4), 1)
        turned = (jnp.where(column < 2, 2 * even, 2 * half) * source) & (length - 1)
        turned = turned.astype(jnp.float32) * (2.0 * math.pi / length)
        cols = jnp.where((column & 1) == 0, jnp.sin(turned), jnp.cos(turned))
        values = matrix_values(length, first, 128, shift_ref[0], tab[...], cols)
        for ref, value in zip(matrices, values):
            ref[rows, :] = value
        return carry

    lax.fori_loop(0, quarter // 128, build, 0)

    def chunk(v, carry):
        own(v).wait()
        for k in (2, 3, 1):
            forth(v, k).wait_recv()
        parts = [land[v, i].reshape(layers * block, sector) for i in range(4)]
        for i, value in enumerate(filter_quarters(parts, tab, matrices)):
            value = value.reshape(layers, block, sector)
            done[v, i] = value
            total = LAYER_WEIGHTS[0] * value[0]
            for layer in range(1, layers):
                total = total + LAYER_WEIGHTS[layer] * value[layer]
            mean = jnp.sum(total.reshape(owned, KR, sector), axis=1) / KR
            for cell in range(owned):
                for tile in range(8):
                    ghost_out[v, i, cell, tile : tile + 1, :] = mean[cell : cell + 1, tile * 128 : (tile + 1) * 128]
        store(v).start()
        ghost_in[v, pl.ds(az * owned, owned)] = ghost_out[v, az]
        for k in (2, 3, 1):
            ghost_back(v, k).start()

        @pl.when(v == variables - 2)
        def _():
            start_back(0, 0)

        return carry

    lax.fori_loop(0, variables, chunk, 0)
    lax.fori_loop(1, variables, start_back, 0)

    def collect(v, carry):
        for k in (2, 3, 1):
            ghost_back(v, k).wait_recv()

        @pl.when(inlet)
        def _():
            ghost[v, pl.ds(0, cells)] = ghost_in[v]

        @pl.when(lower)
        def _():
            ghost_down(v, ax).start()

        return carry

    lax.fori_loop(0, variables, collect, 0)

    @pl.when(inlet)
    def _():
        def arrive(v, carry):
            for source in range(1, axes):
                ghost_down(v, source).wait_recv()
            return carry

        lax.fori_loop(0, variables, arrive, 0)

    for s in range(4):
        receive_halo(s)

        def advance(r, carry):
            for v in range(variables):
                here = [state[s, z, v, r + 1] for z in range(2)]
                below = [jnp.where(inlet, ghost[v, r], under[s, v, r]), here[0]]
                above = [here[1], over[s, v, r]]
                for z in range(2):
                    inward, outward = state[s, z, v, r], state[s, z, v, r + 2]
                    mask = owner_ref[z, r].astype(jnp.float32)
                    rate = mask * (
                        DIFFUSION * (outward + inward + above[z] + below[z] - 4.0 * here[z])
                        - (0.5 * AXIAL_SPEEDS[v]) * (above[z] - below[z])
                        - (0.5 * SWIRL_SPEED) * (outward - inward)
                    )
                    if s == 0:
                        change[z, v, r] = rate
                    elif s < 3:
                        change[z, v, r] = change[z, v, r] + 2.0 * rate
                    start = here[z] if s == 0 else state[0, z, v, r + 1]
                    if s < 3:
                        state[s + 1, z, v, r + 1] = start + (0.5, 0.5, 1.0)[s] * rate
                    else:
                        next_ref[v, r, pl.ds(z, 8, stride=2), :] = start + (change[z, v, r] + rate) / 6.0
            return carry

        lax.fori_loop(0, height, advance, 0)
        if s < 3:
            send_halo(s + 1)

    def finish(v, carry):
        for k in (2, 3, 1):
            forth(v, k).wait_send()
            back(v, k).wait_send()
            back(v, k).wait_recv()
            ghost_back(v, k).wait_send()
        store(v).wait()

        @pl.when(lower)
        def _():
            ghost_down(v, ax).wait_send()

        return carry

    lax.fori_loop(0, variables, finish, 0)
    for s in range(4):
        halo_sent(s)


def whole_step(cycle, field, shift, owner):
    layers, variables, radial, sector = cycle.shape
    _, height, _, _ = field.shape
    length = 4 * sector
    axes = lax.axis_size("ax")
    block = radial // 4
    owned = block // KR
    f32, bf16 = jnp.float32, jnp.bfloat16
    smem = pl.BlockSpec(memory_space=pltpu.SMEM)
    vmem = pl.BlockSpec(memory_space=pltpu.VMEM)
    hbm = pl.BlockSpec(memory_space=pl.ANY)
    dma = pltpu.SemaphoreType.DMA
    woven = (variables, height, 16, 128)
    plane = (variables, height, 8, 128)
    shifted_cycle, stepped = pl.pallas_call(
        lambda *refs: step_body(length, *refs),
        out_shape=[jax.ShapeDtypeStruct(cycle.shape, f32), jax.ShapeDtypeStruct(woven, f32)],
        in_specs=[smem, smem, hbm, hbm],
        out_specs=[hbm, vmem],
        scratch_shapes=[pltpu.VMEM((variables, 4, layers, block, sector), f32)] * 2
        + [pltpu.VMEM((sector, sector), bf16)] * 4
        + [
            pltpu.VMEM((8, sector), f32),
            pltpu.VMEM(woven, f32),
            pltpu.VMEM((4, 2, variables, height + 2, 8, 128), f32),
            pltpu.VMEM((4,) + plane, f32),
            pltpu.VMEM((4,) + plane, f32),
            pltpu.VMEM(plane, f32),
            pltpu.VMEM((variables, 4 * owned, 8, 128), f32),
            pltpu.VMEM((variables, 4, owned, 8, 128), f32),
            pltpu.VMEM((2,) + plane, f32),
        ]
        + [dma((variables, 3))] * 4
        + [dma((variables,))] * 2
        + [dma((1,)), dma((variables, 4)), dma((variables, 4)), dma((variables, axes))]
        + [dma((4, 2))] * 4,
        compiler_params=pltpu.CompilerParams(vmem_limit_bytes=44 * MIB, collective_id=0, has_side_effects=True),
        cost_estimate=pl.CostEstimate(
            flops=24 * layers * variables * radial * sector * sector,
            bytes_accessed=8 * layers * variables * radial * sector,
            transcendentals=0,
        ),
        name="whole_step",
    )(
        shift,
        owner.T,
        cycle,
        pltpu.with_memory_space_constraint(
            field.reshape(variables, height, 2, 8, 128).transpose(0, 1, 3, 2, 4).reshape(woven), pltpu.HBM
        ),
    )
    field_next = stepped.reshape(variables, height, 8, 2, 128).transpose(0, 1, 3, 2, 4).reshape(field.shape)
    return field_next, shifted_cycle


def shifted(array, axis, dim, width):
    devices, length = (lax.axis_size(axis), array.shape[dim])
    up = [(i, (i + 1) % devices) for i in range(devices - 1)]
    down = [(j, i) for i, j in up]
    last = lax.slice_in_dim(array, length - width, length, axis=dim)
    leading = lax.slice_in_dim(array, 0, width, axis=dim)
    return lax.ppermute(last, axis, up), lax.ppermute(leading, axis, down)


def chunked(cycle, shift):
    layers, variables, radial, sector = cycle.shape
    sectors = lax.axis_size("az")
    length = sectors * sector
    shift_value = shift[0]
    tables = shift_tables(shift_value, length)
    matrices = filter_matrices(shift, tables, length)

    def across(part):
        return lax.all_to_all(part, "az", split_axis=0, concat_axis=0, tiled=True)

    def passed(pieces):
        return to_sectors(filtered(to_quarters(pieces), tables, matrices), sectors)

    lead = cycle[:1].reshape(sectors, -1, sector)
    rest = cycle[1:].reshape(sectors, -1, sector)
    lead = across(lead)

    weights = jnp.array(LAYER_WEIGHTS, jnp.float32)
    cells = radial // KR
    grouped = cycle.reshape(layers, variables, cells, KR, sector)
    mean = jnp.sum(jnp.sum(grouped * weights[:, None, None, None, None], axis=0), axis=2) / KR
    around = lax.all_gather(mean.reshape(variables * cells, sector), "az", axis=0, tiled=False)
    lead, around, rest = lax.optimization_barrier((lead, around, rest))
    rest = across(rest)

    ghost = lax.dynamic_index_in_dim(passed(around), lax.axis_index("az"), 0, keepdims=False)

    lead, rest = lax.optimization_barrier((passed(lead), rest))
    lead = across(lead).reshape(1, variables, radial, sector)
    rest = across(passed(rest)).reshape(layers - 1, variables, radial, sector)
    shifted_cycle = jnp.concatenate([lead, rest], axis=0)
    return ghost, shifted_cycle


def on_device(cycle, field, shift, owner):
    layers, variables, radial, sector = cycle.shape
    sectors = lax.axis_size("az")
    if sectors == 4 and sector == 1024 and field.shape[2] == 2 and radial % (4 * KR) == 0:
        return whole_step(cycle, field, shift, owner)
    ghost, shifted_cycle = chunked(cycle, shift)
    ghost = lax.all_gather(ghost.reshape(variables, radial // KR, sector), "ax", axis=1, tiled=True)

    mask = owner.astype(jnp.float32)[None, :, :, None]
    speeds = jnp.array(AXIAL_SPEEDS, jnp.float32)[:, None, None, None]
    at_inlet = lax.axis_index("ax") == 0

    def rates(state):
        inner, outer = shifted(state, "rad", 1, 1)
        under, over = shifted(state, "ax", 2, 1)
        lower = jnp.where(at_inlet, ghost[:, :, None], under)
        outward = jnp.concatenate([state[:, 1:], outer], axis=1)
        inward = jnp.concatenate([inner, state[:, :-1]], axis=1)
        above = jnp.concatenate([state[:, :, 1:], over], axis=2)
        below = jnp.concatenate([lower, state[:, :, :-1]], axis=2)
        return mask * (
            DIFFUSION * (outward + inward + above + below - 4.0 * state)
            - 0.5 * speeds * (above - below)
            - 0.5 * SWIRL_SPEED * (outward - inward)
        )

    first = rates(field)
    second = rates(field + 0.5 * first)
    third = rates(field + 0.5 * second)
    fourth = rates(field + third)
    field_next = field + (first + 2.0 * second + 2.0 * third + fourth) / 6.0
    return (field_next, shifted_cycle)


def solution(mesh):
    in_specs = (P(None, None, ("rad", "ax"), "az"), P(None, "rad", "ax", "az"), P(), P("rad", "ax"))
    out_specs = (P(None, "rad", "ax", "az"), P(None, None, ("rad", "ax"), "az"))
    return jax.shard_map(
        on_device, mesh=mesh, in_specs=in_specs, out_specs=out_specs, check_vma=False
    )
```

```python
import math

import jax
import jax.numpy as jnp
import numpy as np
from jax import lax
from jax.experimental import pallas as pl
from jax.experimental.pallas import tpu as pltpu
from jax.sharding import PartitionSpec as P

KR = 8
LATE = 2
UNROLL = 4


LAYER_WEIGHTS = (0.4, 0.3, 0.2, 0.1)
AXIAL_SPEEDS = (0.35, 0.2, 0.3, 0.25, 0.4)
DIFFUSION = 0.15
SWIRL_SPEED = 0.1
MIB = 1024 * 1024


def class_counts(length):
    top = (length - 1) // 3
    kept = np.arange(-top, top + 1)
    first = kept[kept % 4 == 1]
    assert length % 4 == 0 and (first - 1).sum() == 0
    even, odd, half = [int((kept % 4 == r).sum()) for r in (0, 1, 2)]
    assert even == odd
    return even, half


def shift_tables(shift_value, length):
    quarter = length // 4
    even, half = class_counts(length)
    target = jnp.arange(quarter, dtype=jnp.int32) - shift_value
    rows = []
    for count in (even, half):
        angle = jnp.remainder(count * target, 2 * quarter).astype(jnp.float32) * (math.pi / quarter)
        rows += [jnp.sin(angle), jnp.cos(angle)]
    angle = jnp.remainder(target, length).astype(jnp.float32) * (2.0 * math.pi / length)
    rows += [jnp.cos(angle), jnp.sin(angle)]
    source = np.arange(quarter) * (2.0 * np.pi / length)
    rows += [jnp.asarray(np.cos(source), jnp.float32), jnp.asarray(np.sin(source), jnp.float32)]
    return jnp.stack(rows)


def source_tables(length):
    quarter = length // 4
    source = np.arange(quarter)
    cols = []
    for count in class_counts(length):
        angle = (count * source % (2 * quarter)) * (np.pi / quarter)
        cols += [np.sin(angle), np.cos(angle)]
    return jnp.asarray(np.stack(cols, axis=1), jnp.float32)


def matrix_values(length, first, block, shift_value, rows, cols):
    quarter = length // 4
    even, half = class_counts(length)
    shape = (block, quarter)
    source = lax.broadcasted_iota(jnp.int32, shape, 0) + first
    target = lax.broadcasted_iota(jnp.int32, shape, 1)
    apart = (target - source - shift_value) & (2 * quarter - 1)
    apart = jnp.where(apart >= quarter, apart - 2 * quarter, apart)
    near = jnp.where(apart > quarter // 2, quarter - apart, apart)
    near = jnp.where(apart < -(quarter // 2), -quarter - apart, near)
    u = near.astype(jnp.float32) * (math.pi / quarter)
    w = u * u
    poly = jnp.full(shape, 1.0 / 6227020800.0, jnp.float32)
    for c in (-1.0 / 39916800.0, 1.0 / 362880.0, -1.0 / 5040.0, 1.0 / 120.0, -1.0 / 6.0):
        poly = poly * w + c
    sine = u + u * (w * poly)
    zero = near == 0
    inverse = 0.25 / (quarter * jnp.where(zero, 1.0, sine))
    top_even = rows[0:1, :] * cols[:, 1:2] - rows[1:2, :] * cols[:, 0:1]
    top_half = rows[2:3, :] * cols[:, 3:4] - rows[3:4, :] * cols[:, 2:3]
    sign = jnp.where(apart == 0, 1.0, -1.0)
    m_even = jnp.where(zero, 0.25 * even / quarter, top_even * inverse)
    m_half = jnp.where(zero, sign * (0.25 * half / quarter), top_half * inverse)
    return split(m_even) + split(m_half)


def kernel_matrix_body(length, block, shift_ref, rows_ref, cols_ref, *out_refs):
    first = pl.program_id(0) * block
    values = matrix_values(length, first, block, shift_ref[0], rows_ref[...], cols_ref[...])
    for ref, value in zip(out_refs, values):
        ref[...] = value


def filter_matrices(shift, tables, length):
    quarter = length // 4
    block = 128
    out = jax.ShapeDtypeStruct((quarter, quarter), jnp.bfloat16)
    return pl.pallas_call(
        lambda *refs: kernel_matrix_body(length, block, *refs),
        grid=(quarter // block,),
        out_shape=[out] * 4,
        in_specs=[
            pl.BlockSpec(memory_space=pltpu.SMEM),
            pl.BlockSpec((8, quarter), lambda i: (0, 0)),
            pl.BlockSpec((block, 4), lambda i: (i, 0)),
        ],
        out_specs=[pl.BlockSpec((block, quarter), lambda i: (i, 0))] * 4,
        compiler_params=pltpu.CompilerParams(vmem_limit_bytes=32 * MIB),
        cost_estimate=pl.CostEstimate(flops=60 * quarter * quarter, bytes_accessed=8 * quarter * quarter, transcendentals=0),
        name="filter_matrices",
    )(shift, tables, source_tables(length))


def split(value):
    high = value.astype(jnp.bfloat16)
    return high, (value - high.astype(jnp.float32)).astype(jnp.bfloat16)


def product(value, high_ref, low_ref):
    high, low = split(value)
    f32 = jnp.float32
    return (
        jnp.dot(high, low_ref[...], preferred_element_type=f32)
        + jnp.dot(low, high_ref[...], preferred_element_type=f32)
        + jnp.dot(high, high_ref[...], preferred_element_type=f32)
    )


def filter_quarters(parts, tab_ref, matrix_refs):
    x0, x1, x2, x3 = parts
    count = x0.shape[0]
    eh_ref, el_ref, hh_ref, hl_ref = matrix_refs
    cos_t, sin_t = 2.0 * tab_ref[4:5, :], 2.0 * tab_ref[5:6, :]
    cos_s, sin_s = tab_ref[6:7, :], tab_ref[7:8, :]
    even, odd = x0 + x2, x1 + x3
    re, im = x0 - x2, x3 - x1
    stacked = jnp.concatenate([even + odd, re * cos_s + im * sin_s, im * cos_s - re * sin_s], axis=0)
    turned = product(stacked, eh_ref, el_ref)
    z2 = product(even - odd, hh_ref, hl_ref)
    z0, ure, uim = turned[:count], turned[count : 2 * count], turned[2 * count :]
    zre = cos_t * ure - sin_t * uim
    zim = cos_t * uim + sin_t * ure
    plus, minus = z0 + z2, z0 - z2
    return plus + zre, minus - zim, plus - zre, minus + zim


def filter_body(x_ref, tab_ref, eh_ref, el_ref, hh_ref, hl_ref, out_ref):
    values = filter_quarters([x_ref[i] for i in range(4)], tab_ref, (eh_ref, el_ref, hh_ref, hl_ref))
    for i, value in enumerate(values):
        out_ref[i] = value


def filtered(quarters, tables, matrices):
    _, count, quarter = quarters.shape
    block = next((b for b in (80, 64, 40, 32, 16, 8) if count % b == 0), count)
    whole = pl.BlockSpec((quarter, quarter), lambda i: (0, 0))
    part = pl.BlockSpec((4, block, quarter), lambda i: (0, i, 0))
    return pl.pallas_call(
        filter_body,
        grid=(count // block,),
        out_shape=jax.ShapeDtypeStruct(quarters.shape, jnp.float32),
        in_specs=[part, pl.BlockSpec((8, quarter), lambda i: (0, 0))] + [whole] * 4,
        out_specs=part,
        compiler_params=pltpu.CompilerParams(vmem_limit_bytes=48 * MIB),
        cost_estimate=pl.CostEstimate(
            flops=24 * count * quarter * quarter,
            bytes_accessed=32 * count * quarter + 8 * quarter * quarter,
            transcendentals=0,
        ),
        name="spectral_filter",
    )(quarters, tables, *matrices)


def to_quarters(pieces):
    sectors, count, sector = pieces.shape
    per = sectors // 4
    if per == 1:
        return pieces
    return pieces.reshape(4, per, count, sector).transpose(0, 2, 1, 3).reshape(4, count, per * sector)


def to_sectors(quarters, sectors):
    _, count, quarter = quarters.shape
    per = sectors // 4
    if per == 1:
        return quarters
    sector = quarter // per
    return quarters.reshape(4, count, per, sector).transpose(0, 2, 1, 3).reshape(sectors, count, sector)


def step_body(length, shift_ref, owner_hbm, cycle_ref, field_ref, out_ref, next_ref,
              owner_ref, land, done, eh, el, hh, hl, tab, loaded, state, under, over, ghost, ghost_in, ghost_out, change,
              send_sem, recv_sem, back_send, back_recv, own_sem, store_sem, load_sem,
              ghost_send, ghost_recv, inlet_recv, axial_send, axial_recv, radial_send, radial_recv):
    layers, variables, radial, sector = cycle_ref.shape
    quarter = length // 4
    block = radial // 4
    owned = block // KR
    cells = radial // KR
    height = next_ref.shape[1]
    az, rad, ax = lax.axis_index("az"), lax.axis_index("rad"), lax.axis_index("ax")
    rads, axes = lax.axis_size("rad"), lax.axis_size("ax")
    inner, outer = rad > 0, rad < rads - 1
    inlet, lower, upper = ax == 0, ax > 0, ax < axes - 1
    late = min(LATE, variables)
    matrices = (eh, el, hh, hl)
    mesh_id = pl.DeviceIdType.MESH

    barrier = pltpu.get_barrier_semaphore()
    for peer in [{"az": lax.rem(az + i, 4)} for i in (1, 2, 3)] + [{"ax": lax.rem(ax + j, axes)} for j in range(1, axes)]:
        pl.semaphore_signal(barrier, inc=1, device_id=peer, device_id_type=mesh_id)

    @pl.when(inner)
    def _():
        pl.semaphore_signal(barrier, inc=1, device_id={"rad": rad - 1}, device_id_type=mesh_id)

    @pl.when(outer)
    def _():
        pl.semaphore_signal(barrier, inc=1, device_id={"rad": rad + 1}, device_id_type=mesh_id)

    pl.semaphore_wait(barrier, axes + 2 + inner.astype(jnp.int32) + outer.astype(jnp.int32))

    def partner(k):
        return (None, az + 1 - 2 * lax.rem(az, 2), lax.rem(az + 2, 4), 3 - az)[k]

    def rows_of(index):
        return pl.ds(pl.multiple_of(index * block, block), block)

    def remote(src, dst, send, recv, peer):
        return pltpu.make_async_remote_copy(
            src_ref=src, dst_ref=dst, send_sem=send, recv_sem=recv, device_id=peer, device_id_type=mesh_id
        )

    def forth(v, k):
        peer = partner(k)
        return remote(
            cycle_ref.at[:, v, rows_of(peer)], land.at[v, az], send_sem.at[v, k - 1], recv_sem.at[v, k - 1], {"az": peer}
        )

    def back(v, k):
        peer = partner(k)
        return remote(
            done.at[v, peer], out_ref.at[:, v, rows_of(az)], back_send.at[v, k - 1], back_recv.at[v, k - 1], {"az": peer}
        )

    def own(v):
        return pltpu.make_async_copy(cycle_ref.at[:, v, rows_of(az)], land.at[v, az], own_sem.at[v])

    def store(v):
        return pltpu.make_async_copy(done.at[v, az], out_ref.at[:, v, rows_of(az)], store_sem.at[v])

    def ghost_back(v, k):
        peer = partner(k)
        return remote(
            ghost_out.at[v, peer], ghost_in.at[v, pl.ds(az * owned, owned)],
            ghost_send.at[v, k], ghost_recv.at[v, k], {"az": peer},
        )

    def ghost_down(v, source):
        return remote(
            ghost_in.at[v], ghost.at[v, pl.ds(source * cells, cells)],
            ghost_send.at[v, 0], inlet_recv.at[v, source], {"ax": 0},
        )

    def raise_copy(s, v):
        return remote(state.at[s, 1, v, pl.ds(1, height)], under.at[s, v], axial_send.at[s, v, 0], axial_recv.at[s, v, 0], {"ax": ax + 1})

    def lower_copy(s, v):
        return remote(state.at[s, 0, v, pl.ds(1, height)], over.at[s, v], axial_send.at[s, v, 1], axial_recv.at[s, v, 1], {"ax": ax - 1})

    def outward_copy(s, v):
        return remote(state.at[s, :, v, height], state.at[s, :, v, 0], radial_send.at[s, v, 0], radial_recv.at[s, v, 0], {"rad": rad + 1})

    def inward_copy(s, v):
        return remote(state.at[s, :, v, 1], state.at[s, :, v, height + 1], radial_send.at[s, v, 1], radial_recv.at[s, v, 1], {"rad": rad - 1})

    def send_halo(s, v):
        for there, copy in ((upper, raise_copy), (lower, lower_copy), (outer, outward_copy), (inner, inward_copy)):
            @pl.when(there)
            def _():
                copy(s, v).start()

    def receive_halo(s, v):
        for there, copy in ((lower, raise_copy), (upper, lower_copy), (inner, outward_copy), (outer, inward_copy)):
            @pl.when(there)
            def _():
                copy(s, v).wait_recv()

    def halo_sent(s, v):
        for there, copy in ((upper, raise_copy), (lower, lower_copy), (outer, outward_copy), (inner, inward_copy)):
            @pl.when(there)
            def _():
                copy(s, v).wait_send()

    def average(parts, ref):
        total = LAYER_WEIGHTS[0] * parts[0]
        for layer in range(1, layers):
            total = total + LAYER_WEIGHTS[layer] * parts[layer]
        mean = jnp.sum(total, axis=0, keepdims=True) / KR
        for tile in range(8):
            ref[tile : tile + 1, :] = mean[:, tile * 128 : (tile + 1) * 128]

    def start_forth(v, carry):
        for k in (2, 3, 1):
            forth(v, k).start()
        own(v).start()
        return carry

    def start_back(v, carry):
        for k in (2, 3, 1):
            back(v, k).start()
        return carry

    loads = [
        pltpu.make_async_copy(src, dst, load_sem.at[i])
        for i, (src, dst) in enumerate(((field_ref, loaded), (owner_hbm, owner_ref)))
    ]
    lax.fori_loop(0, variables, start_forth, 0)
    for load in loads:
        load.start()
    for load in loads:
        load.wait()

    @pl.when(jnp.logical_not(upper))
    def _():
        over[...] = jnp.zeros_like(over)

    @pl.when(jnp.logical_not(inner))
    def _():
        state[:, :, :, 0] = jnp.zeros((4, 2, variables, 8, 128), jnp.float32)

    @pl.when(jnp.logical_not(outer))
    def _():
        state[:, :, :, height + 1] = jnp.zeros((4, 2, variables, 8, 128), jnp.float32)

    def unweave(r, carry):
        for v in range(variables):
            for z in range(2):
                state[0, z, v, r + 1] = loaded[v, r, pl.ds(z, 8, stride=2), :]
        return carry

    lax.fori_loop(0, height, unweave, 0)

    def first_halo(v, carry):
        send_halo(0, v)
        return carry

    lax.fori_loop(0, variables, first_halo, 0)

    even, half = class_counts(length)
    row = lax.broadcasted_iota(jnp.int32, (8, quarter), 0)
    target = lax.broadcasted_iota(jnp.int32, (8, quarter), 1)
    count = jnp.where(row < 2, 2 * even, jnp.where(row < 4, 2 * half, 1))
    angle = (count * (target - jnp.where(row < 6, shift_ref[0], 0))) & (length - 1)
    angle = angle.astype(jnp.float32) * (2.0 * math.pi / length)
    sines = (row == 0) | (row == 2) | (row == 5) | (row == 7)
    tab[...] = jnp.where(sines, jnp.sin(angle), jnp.cos(angle))

    def build(i, carry):
        first = pl.multiple_of(i * 128, 128)
        rows = pl.ds(first, 128)
        source = lax.broadcasted_iota(jnp.int32, (128, 4), 0) + first
        column = lax.broadcasted_iota(jnp.int32, (128, 4), 1)
        turned = (jnp.where(column < 2, 2 * even, 2 * half) * source) & (length - 1)
        turned = turned.astype(jnp.float32) * (2.0 * math.pi / length)
        cols = jnp.where((column & 1) == 0, jnp.sin(turned), jnp.cos(turned))
        values = matrix_values(length, first, 128, shift_ref[0], tab[...], cols)
        for ref, value in zip(matrices, values):
            ref[rows, :] = value
        return carry

    lax.fori_loop(0, quarter // 128, build, 0)

    def chunk(v, carry):
        own(v).wait()
        for k in (2, 3, 1):
            forth(v, k).wait_recv()
        parts = [land[v, i].reshape(layers * block, sector) for i in range(4)]
        for i, value in enumerate(filter_quarters(parts, tab, matrices)):
            done[v, i] = value.reshape(layers, block, sector)
        store(v).start()

        @pl.when(v >= variables - late)
        def _():
            for i in range(4):
                for cell in range(owned):
                    rows = slice(cell * KR, (cell + 1) * KR)
                    average([done[v, i, layer, rows, :] for layer in range(layers)], ghost_out.at[v, i, cell])
            ghost_in[v, pl.ds(az * owned, owned)] = ghost_out[v, az]
            for k in (2, 3, 1):
                ghost_back(v, k).start()

        @pl.when(v == variables - 2)
        def _():
            start_back(0, 0)

        return carry

    lax.fori_loop(0, variables, chunk, 0)
    lax.fori_loop(1, variables, start_back, 0)

    def gather(v):
        @pl.when(lower)
        def _():
            ghost_down(v, ax).start()

        @pl.when(inlet)
        def _():
            ghost[v, pl.ds(0, cells)] = ghost_in[v]

    def sent_ghost(v, carry):
        for k in (2, 3, 1):
            ghost_back(v, k).wait_recv()
        gather(v)
        return carry

    def own_ghost(v, carry):
        def local(cell, carry):
            rows = pl.ds(pl.multiple_of(cell * KR, KR), KR)
            average([out_ref[layer, v, rows, :] for layer in range(layers)], ghost_in.at[v, cell])
            return carry

        lax.fori_loop(0, cells, local, 0)
        gather(v)
        return carry

    def evolve(first, last):
        @pl.when(inlet)
        def _():
            def arrive(v, carry):
                for source in range(1, axes):
                    ghost_down(v, source).wait_recv()
                return carry

            lax.fori_loop(first, last, arrive, 0)

        for s in range(4):
            def stage(v, carry):
                receive_halo(s, v)
                speed = sum(jnp.where(v == i, 0.5 * value, 0.0) for i, value in enumerate(AXIAL_SPEEDS))

                def advance(r, carry):
                    here = [state[s, z, v, r + 1] for z in range(2)]
                    below = [jnp.where(inlet, ghost[v, r], under[s, v, r]), here[0]]
                    above = [here[1], over[s, v, r]]
                    for z in range(2):
                        inward, outward = state[s, z, v, r], state[s, z, v, r + 2]
                        mask = owner_ref[z, r].astype(jnp.float32)
                        rate = mask * (
                            DIFFUSION * (outward + inward + above[z] + below[z] - 4.0 * here[z])
                            - speed * (above[z] - below[z])
                            - (0.5 * SWIRL_SPEED) * (outward - inward)
                        )
                        if s == 0:
                            change[z, v, r] = rate
                        elif s < 3:
                            change[z, v, r] = change[z, v, r] + 2.0 * rate
                        start = here[z] if s == 0 else state[0, z, v, r + 1]
                        if s < 3:
                            state[s + 1, z, v, r + 1] = start + (0.5, 0.5, 1.0)[s] * rate
                        else:
                            next_ref[v, r, pl.ds(z, 8, stride=2), :] = start + (change[z, v, r] + rate) / 6.0
                    return carry

                lax.fori_loop(0, height, advance, 0, unroll=UNROLL)
                if s < 3:
                    send_halo(s + 1, v)
                return carry

            lax.fori_loop(first, last, stage, 0)

    lax.fori_loop(variables - late, variables, sent_ghost, 0)
    evolve(variables - late, variables)
    for v in range(variables - late):
        for k in (2, 3, 1):
            back(v, k).wait_recv()
        store(v).wait()
        own_ghost(v, 0)
    evolve(0, variables - late)

    def finish(v, carry):
        for s in range(4):
            halo_sent(s, v)
        for k in (2, 3, 1):
            forth(v, k).wait_send()

        @pl.when(lower)
        def _():
            ghost_down(v, ax).wait_send()

        @pl.when(v >= variables - late)
        def _():
            for k in (2, 3, 1):
                ghost_back(v, k).wait_send()
            store(v).wait()

        return carry

    lax.fori_loop(0, variables, finish, 0)

    def returned(v, carry):
        for k in (2, 3, 1):
            back(v, k).wait_send()

        @pl.when(v >= variables - late)
        def _():
            for k in (2, 3, 1):
                back(v, k).wait_recv()

        return carry

    lax.fori_loop(0, variables, returned, 0)


def whole_step(cycle, field, shift, owner):
    layers, variables, radial, sector = cycle.shape
    _, height, _, _ = field.shape
    length = 4 * sector
    axes = lax.axis_size("ax")
    block = radial // 4
    owned = block // KR
    f32, bf16 = jnp.float32, jnp.bfloat16
    smem = pl.BlockSpec(memory_space=pltpu.SMEM)
    vmem = pl.BlockSpec(memory_space=pltpu.VMEM)
    hbm = pl.BlockSpec(memory_space=pl.ANY)
    dma = pltpu.SemaphoreType.DMA
    woven = (variables, height, 16, 128)
    plane = (variables, height, 8, 128)
    shifted_cycle, stepped = pl.pallas_call(
        lambda *refs: step_body(length, *refs),
        out_shape=[pltpu.VMEM(cycle.shape, f32), pltpu.VMEM(woven, f32)],
        in_specs=[smem, hbm, hbm, hbm],
        out_specs=[vmem, vmem],
        scratch_shapes=[pltpu.SMEM(owner.T.shape, jnp.int32)]
        + [pltpu.VMEM((variables, 4, layers, block, sector), f32)] * 2
        + [pltpu.VMEM((sector, sector), bf16)] * 4
        + [
            pltpu.VMEM((8, sector), f32),
            pltpu.VMEM(woven, f32),
            pltpu.VMEM((4, 2, variables, height + 2, 8, 128), f32),
            pltpu.VMEM((4,) + plane, f32),
            pltpu.VMEM((4,) + plane, f32),
            pltpu.VMEM(plane, f32),
            pltpu.VMEM((variables, 4 * owned, 8, 128), f32),
            pltpu.VMEM((variables, 4, owned, 8, 128), f32),
            pltpu.VMEM((2,) + plane, f32),
        ]
        + [dma((variables, 3))] * 4
        + [dma((variables,))] * 2
        + [dma((2,)), dma((variables, 4)), dma((variables, 4)), dma((variables, axes))]
        + [dma((4, variables, 2))] * 4,
        compiler_params=pltpu.CompilerParams(vmem_limit_bytes=44 * MIB, collective_id=0, has_side_effects=True),
        cost_estimate=pl.CostEstimate(
            flops=24 * layers * variables * radial * sector * sector,
            bytes_accessed=8 * layers * variables * radial * sector,
            transcendentals=0,
        ),
        name="whole_step",
    )(
        shift,
        pltpu.with_memory_space_constraint(owner.T, pltpu.HBM),
        cycle,
        pltpu.with_memory_space_constraint(
            field.reshape(variables, height, 2, 8, 128).transpose(0, 1, 3, 2, 4).reshape(woven), pltpu.HBM
        ),
    )
    shifted_cycle, stepped = written(shifted_cycle, stepped)
    field_next = stepped.reshape(variables, height, 8, 2, 128).transpose(0, 1, 3, 2, 4).reshape(field.shape)
    return field_next, shifted_cycle


def shifted(array, axis, dim, width):
    devices, length = (lax.axis_size(axis), array.shape[dim])
    up = [(i, (i + 1) % devices) for i in range(devices - 1)]
    down = [(j, i) for i, j in up]
    last = lax.slice_in_dim(array, length - width, length, axis=dim)
    leading = lax.slice_in_dim(array, 0, width, axis=dim)
    return lax.ppermute(last, axis, up), lax.ppermute(leading, axis, down)


def chunked(cycle, shift):
    layers, variables, radial, sector = cycle.shape
    sectors = lax.axis_size("az")
    length = sectors * sector
    shift_value = shift[0]
    tables = shift_tables(shift_value, length)
    matrices = filter_matrices(shift, tables, length)

    def across(part):
        return lax.all_to_all(part, "az", split_axis=0, concat_axis=0, tiled=True)

    def passed(pieces):
        return to_sectors(filtered(to_quarters(pieces), tables, matrices), sectors)

    lead = cycle[:1].reshape(sectors, -1, sector)
    rest = cycle[1:].reshape(sectors, -1, sector)
    lead = across(lead)

    weights = jnp.array(LAYER_WEIGHTS, jnp.float32)
    cells = radial // KR
    grouped = cycle.reshape(layers, variables, cells, KR, sector)
    mean = jnp.sum(jnp.sum(grouped * weights[:, None, None, None, None], axis=0), axis=2) / KR
    around = lax.all_gather(mean.reshape(variables * cells, sector), "az", axis=0, tiled=False)
    lead, around, rest = lax.optimization_barrier((lead, around, rest))
    rest = across(rest)

    ghost = lax.dynamic_index_in_dim(passed(around), lax.axis_index("az"), 0, keepdims=False)

    lead, rest = lax.optimization_barrier((passed(lead), rest))
    lead = across(lead).reshape(1, variables, radial, sector)
    rest = across(passed(rest)).reshape(layers - 1, variables, radial, sector)
    shifted_cycle = jnp.concatenate([lead, rest], axis=0)
    return ghost, shifted_cycle


def write_body(cycle_ref, field_ref, cycle_out, field_out, sems):
    layers = cycle_ref.shape[0]
    copies = [pltpu.make_async_copy(cycle_ref.at[i], cycle_out.at[i], sems.at[i]) for i in range(layers)]
    copies.append(pltpu.make_async_copy(field_ref, field_out, sems.at[layers]))
    for copy in copies:
        copy.start()
    for copy in copies:
        copy.wait()


def written(cycle, field):
    vmem = pl.BlockSpec(memory_space=pltpu.VMEM)
    hbm = pl.BlockSpec(memory_space=pltpu.HBM)
    return pl.pallas_call(
        write_body,
        out_shape=[pltpu.HBM(cycle.shape, cycle.dtype), pltpu.HBM(field.shape, field.dtype)],
        in_specs=[vmem, vmem],
        out_specs=[hbm, hbm],
        scratch_shapes=[pltpu.SemaphoreType.DMA((cycle.shape[0] + 1,))],
        compiler_params=pltpu.CompilerParams(vmem_limit_bytes=4 * MIB),
        name="write_results",
    )(cycle, field)


def on_device(cycle, field, shift, owner):
    layers, variables, radial, sector = cycle.shape
    sectors = lax.axis_size("az")
    if sectors == 4 and sector == 1024 and field.shape[2] == 2 and radial % (4 * KR) == 0:
        return whole_step(cycle, field, shift, owner)
    ghost, shifted_cycle = chunked(cycle, shift)
    ghost = lax.all_gather(ghost.reshape(variables, radial // KR, sector), "ax", axis=1, tiled=True)

    mask = owner.astype(jnp.float32)[None, :, :, None]
    speeds = jnp.array(AXIAL_SPEEDS, jnp.float32)[:, None, None, None]
    at_inlet = lax.axis_index("ax") == 0

    def rates(state):
        inner, outer = shifted(state, "rad", 1, 1)
        under, over = shifted(state, "ax", 2, 1)
        lower = jnp.where(at_inlet, ghost[:, :, None], under)
        outward = jnp.concatenate([state[:, 1:], outer], axis=1)
        inward = jnp.concatenate([inner, state[:, :-1]], axis=1)
        above = jnp.concatenate([state[:, :, 1:], over], axis=2)
        below = jnp.concatenate([lower, state[:, :, :-1]], axis=2)
        return mask * (
            DIFFUSION * (outward + inward + above + below - 4.0 * state)
            - 0.5 * speeds * (above - below)
            - 0.5 * SWIRL_SPEED * (outward - inward)
        )

    first = rates(field)
    second = rates(field + 0.5 * first)
    third = rates(field + 0.5 * second)
    fourth = rates(field + third)
    field_next = field + (first + 2.0 * second + 2.0 * third + fourth) / 6.0
    return (field_next, shifted_cycle)


def solution(mesh):
    in_specs = (P(None, None, ("rad", "ax"), "az"), P(None, "rad", "ax", "az"), P(), P("rad", "ax"))
    out_specs = (P(None, "rad", "ax", "az"), P(None, None, ("rad", "ax"), "az"))
    return jax.shard_map(
        on_device, mesh=mesh, in_specs=in_specs, out_specs=out_specs, check_vma=False
    )
```

```python
import math

import jax
import jax.numpy as jnp
import numpy as np
from jax import lax
from jax.experimental import pallas as pl
from jax.experimental.pallas import tpu as pltpu
from jax.sharding import PartitionSpec as P

KR = 8
LATE = 2
UNROLL = 4


LAYER_WEIGHTS = (0.4, 0.3, 0.2, 0.1)
AXIAL_SPEEDS = (0.35, 0.2, 0.3, 0.25, 0.4)
DIFFUSION = 0.15
SWIRL_SPEED = 0.1
MIB = 1024 * 1024


def class_counts(length):
    top = (length - 1) // 3
    kept = np.arange(-top, top + 1)
    first = kept[kept % 4 == 1]
    assert length % 4 == 0 and (first - 1).sum() == 0
    even, odd, half = [int((kept % 4 == r).sum()) for r in (0, 1, 2)]
    assert even == odd
    return even, half


def shift_tables(shift_value, length):
    quarter = length // 4
    even, half = class_counts(length)
    target = jnp.arange(quarter, dtype=jnp.int32) - shift_value
    rows = []
    for count in (even, half):
        angle = jnp.remainder(count * target, 2 * quarter).astype(jnp.float32) * (math.pi / quarter)
        rows += [jnp.sin(angle), jnp.cos(angle)]
    angle = jnp.remainder(target, length).astype(jnp.float32) * (2.0 * math.pi / length)
    rows += [jnp.cos(angle), jnp.sin(angle)]
    source = np.arange(quarter) * (2.0 * np.pi / length)
    rows += [jnp.asarray(np.cos(source), jnp.float32), jnp.asarray(np.sin(source), jnp.float32)]
    return jnp.stack(rows)


def source_tables(length):
    quarter = length // 4
    source = np.arange(quarter)
    cols = []
    for count in class_counts(length):
        angle = (count * source % (2 * quarter)) * (np.pi / quarter)
        cols += [np.sin(angle), np.cos(angle)]
    return jnp.asarray(np.stack(cols, axis=1), jnp.float32)


def matrix_values(length, first, block, shift_value, rows, cols):
    quarter = length // 4
    even, half = class_counts(length)
    shape = (block, quarter)
    source = lax.broadcasted_iota(jnp.int32, shape, 0) + first
    target = lax.broadcasted_iota(jnp.int32, shape, 1)
    apart = (target - source - shift_value) & (2 * quarter - 1)
    apart = jnp.where(apart >= quarter, apart - 2 * quarter, apart)
    near = jnp.where(apart > quarter // 2, quarter - apart, apart)
    near = jnp.where(apart < -(quarter // 2), -quarter - apart, near)
    u = near.astype(jnp.float32) * (math.pi / quarter)
    w = u * u
    poly = jnp.full(shape, 1.0 / 6227020800.0, jnp.float32)
    for c in (-1.0 / 39916800.0, 1.0 / 362880.0, -1.0 / 5040.0, 1.0 / 120.0, -1.0 / 6.0):
        poly = poly * w + c
    sine = u + u * (w * poly)
    zero = near == 0
    inverse = 0.25 / (quarter * jnp.where(zero, 1.0, sine))
    top_even = rows[0:1, :] * cols[:, 1:2] - rows[1:2, :] * cols[:, 0:1]
    top_half = rows[2:3, :] * cols[:, 3:4] - rows[3:4, :] * cols[:, 2:3]
    sign = jnp.where(apart == 0, 1.0, -1.0)
    m_even = jnp.where(zero, 0.25 * even / quarter, top_even * inverse)
    m_half = jnp.where(zero, sign * (0.25 * half / quarter), top_half * inverse)
    return split(m_even) + split(m_half)


def kernel_matrix_body(length, block, shift_ref, rows_ref, cols_ref, *out_refs):
    first = pl.program_id(0) * block
    values = matrix_values(length, first, block, shift_ref[0], rows_ref[...], cols_ref[...])
    for ref, value in zip(out_refs, values):
        ref[...] = value


def filter_matrices(shift, tables, length):
    quarter = length // 4
    block = 128
    out = jax.ShapeDtypeStruct((quarter, quarter), jnp.bfloat16)
    return pl.pallas_call(
        lambda *refs: kernel_matrix_body(length, block, *refs),
        grid=(quarter // block,),
        out_shape=[out] * 4,
        in_specs=[
            pl.BlockSpec(memory_space=pltpu.SMEM),
            pl.BlockSpec((8, quarter), lambda i: (0, 0)),
            pl.BlockSpec((block, 4), lambda i: (i, 0)),
        ],
        out_specs=[pl.BlockSpec((block, quarter), lambda i: (i, 0))] * 4,
        compiler_params=pltpu.CompilerParams(vmem_limit_bytes=32 * MIB),
        cost_estimate=pl.CostEstimate(flops=60 * quarter * quarter, bytes_accessed=8 * quarter * quarter, transcendentals=0),
        name="filter_matrices",
    )(shift, tables, source_tables(length))


def split(value):
    high = value.astype(jnp.bfloat16)
    return high, (value - high.astype(jnp.float32)).astype(jnp.bfloat16)


def product(value, high_ref, low_ref):
    high, low = split(value)
    f32 = jnp.float32
    return (
        jnp.dot(high, low_ref[...], preferred_element_type=f32)
        + jnp.dot(low, high_ref[...], preferred_element_type=f32)
        + jnp.dot(high, high_ref[...], preferred_element_type=f32)
    )


def filter_quarters(parts, tab_ref, matrix_refs):
    x0, x1, x2, x3 = parts
    count = x0.shape[0]
    eh_ref, el_ref, hh_ref, hl_ref = matrix_refs
    cos_t, sin_t = 2.0 * tab_ref[4:5, :], 2.0 * tab_ref[5:6, :]
    cos_s, sin_s = tab_ref[6:7, :], tab_ref[7:8, :]
    even, odd = x0 + x2, x1 + x3
    re, im = x0 - x2, x3 - x1
    stacked = jnp.concatenate([even + odd, re * cos_s + im * sin_s, im * cos_s - re * sin_s], axis=0)
    turned = product(stacked, eh_ref, el_ref)
    z2 = product(even - odd, hh_ref, hl_ref)
    z0, ure, uim = turned[:count], turned[count : 2 * count], turned[2 * count :]
    zre = cos_t * ure - sin_t * uim
    zim = cos_t * uim + sin_t * ure
    plus, minus = z0 + z2, z0 - z2
    return plus + zre, minus - zim, plus - zre, minus + zim


def filter_body(x_ref, tab_ref, eh_ref, el_ref, hh_ref, hl_ref, out_ref):
    values = filter_quarters([x_ref[i] for i in range(4)], tab_ref, (eh_ref, el_ref, hh_ref, hl_ref))
    for i, value in enumerate(values):
        out_ref[i] = value


def filtered(quarters, tables, matrices):
    _, count, quarter = quarters.shape
    block = next((b for b in (80, 64, 40, 32, 16, 8) if count % b == 0), count)
    whole = pl.BlockSpec((quarter, quarter), lambda i: (0, 0))
    part = pl.BlockSpec((4, block, quarter), lambda i: (0, i, 0))
    return pl.pallas_call(
        filter_body,
        grid=(count // block,),
        out_shape=jax.ShapeDtypeStruct(quarters.shape, jnp.float32),
        in_specs=[part, pl.BlockSpec((8, quarter), lambda i: (0, 0))] + [whole] * 4,
        out_specs=part,
        compiler_params=pltpu.CompilerParams(vmem_limit_bytes=48 * MIB),
        cost_estimate=pl.CostEstimate(
            flops=24 * count * quarter * quarter,
            bytes_accessed=32 * count * quarter + 8 * quarter * quarter,
            transcendentals=0,
        ),
        name="spectral_filter",
    )(quarters, tables, *matrices)


def to_quarters(pieces):
    sectors, count, sector = pieces.shape
    per = sectors // 4
    if per == 1:
        return pieces
    return pieces.reshape(4, per, count, sector).transpose(0, 2, 1, 3).reshape(4, count, per * sector)


def to_sectors(quarters, sectors):
    _, count, quarter = quarters.shape
    per = sectors // 4
    if per == 1:
        return quarters
    sector = quarter // per
    return quarters.reshape(4, count, per, sector).transpose(0, 2, 1, 3).reshape(sectors, count, sector)


def step_body(length, shift_ref, owner_hbm, cycle_ref, field_ref, out_ref, next_ref,
              owner_ref, land, done, eh, el, hh, hl, tab, loaded, state, under, over, ghost, ghost_in, ghost_out, change,
              send_sem, recv_sem, back_send, back_recv, own_sem, store_sem, load_sem,
              ghost_send, ghost_recv, down_send, inlet_recv, axial_send, axial_recv, radial_send, radial_recv):
    layers, variables, radial, sector = cycle_ref.shape
    quarter = length // 4
    block = radial // 4
    owned = block // KR
    cells = radial // KR
    height = next_ref.shape[1]
    az, rad, ax = lax.axis_index("az"), lax.axis_index("rad"), lax.axis_index("ax")
    rads, axes = lax.axis_size("rad"), lax.axis_size("ax")
    inner, outer = rad > 0, rad < rads - 1
    inlet, lower, upper = ax == 0, ax > 0, ax < axes - 1
    late = min(LATE, variables)
    matrices = (eh, el, hh, hl)
    mesh_id = pl.DeviceIdType.MESH

    barrier = pltpu.get_barrier_semaphore()
    for peer in [{"az": lax.rem(az + i, 4)} for i in (1, 2, 3)] + [{"ax": lax.rem(ax + j, axes)} for j in range(1, axes)]:
        pl.semaphore_signal(barrier, inc=1, device_id=peer, device_id_type=mesh_id)

    @pl.when(inner)
    def _():
        pl.semaphore_signal(barrier, inc=1, device_id={"rad": rad - 1}, device_id_type=mesh_id)

    @pl.when(outer)
    def _():
        pl.semaphore_signal(barrier, inc=1, device_id={"rad": rad + 1}, device_id_type=mesh_id)

    pl.semaphore_wait(barrier, axes + 2 + inner.astype(jnp.int32) + outer.astype(jnp.int32))

    def partner(k):
        return (None, az + 1 - 2 * lax.rem(az, 2), lax.rem(az + 2, 4), 3 - az)[k]

    def rows_of(index):
        return pl.ds(pl.multiple_of(index * block, block), block)

    def remote(src, dst, send, recv, peer):
        return pltpu.make_async_remote_copy(
            src_ref=src, dst_ref=dst, send_sem=send, recv_sem=recv, device_id=peer, device_id_type=mesh_id
        )

    def forth(v, k):
        peer = partner(k)
        return remote(
            cycle_ref.at[:, v, rows_of(peer)], land.at[v, az], send_sem.at[0], recv_sem.at[v], {"az": peer}
        )

    def back(v, k):
        peer = partner(k)
        return remote(
            done.at[v, peer], out_ref.at[:, v, rows_of(az)], back_send.at[0], back_recv.at[v], {"az": peer}
        )

    def own(v):
        return pltpu.make_async_copy(cycle_ref.at[:, v, rows_of(az)], land.at[v, az], own_sem.at[v])

    def store(v):
        return pltpu.make_async_copy(done.at[v, az], out_ref.at[:, v, rows_of(az)], store_sem.at[v])

    def arrived(ref, semaphore):
        remote(ref, ref, semaphore, semaphore, {"az": partner(1)}).wait_recv()

    def left(ref, semaphore):
        remote(ref, ref, semaphore, semaphore, {"az": partner(1)}).wait_send()

    def ghost_back(v, k):
        peer = partner(k)
        return remote(
            ghost_out.at[v, peer], ghost_in.at[v, pl.ds(az * owned, owned)], ghost_send.at[0], ghost_recv.at[v], {"az": peer}
        )

    def ghost_down(v, group):
        return remote(
            ghost_in.at[v], ghost.at[v, pl.ds(ax * cells, cells)], down_send.at[0], inlet_recv.at[group], {"ax": 0}
        )

    def send_halo(s, v, group):
        @pl.when(upper)
        def _():
            remote(
                state.at[s, 1, v, pl.ds(1, height)], under.at[s, v], axial_send.at[0], axial_recv.at[s, group, 0], {"ax": ax + 1}
            ).start()

        @pl.when(lower)
        def _():
            remote(
                state.at[s, 0, v, pl.ds(1, height)], over.at[s, v], axial_send.at[1], axial_recv.at[s, group, 1], {"ax": ax - 1}
            ).start()

        @pl.when(outer)
        def _():
            remote(
                state.at[s, :, v, height], state.at[s, :, v, 0], radial_send.at[0], radial_recv.at[s, group, 0], {"rad": rad + 1}
            ).start()

        @pl.when(inner)
        def _():
            remote(
                state.at[s, :, v, 1], state.at[s, :, v, height + 1], radial_send.at[1], radial_recv.at[s, group, 1], {"rad": rad - 1}
            ).start()

    def receive_halo(s, part, group):
        @pl.when(lower)
        def _():
            arrived(under.at[s, part], axial_recv.at[s, group, 0])

        @pl.when(upper)
        def _():
            arrived(over.at[s, part], axial_recv.at[s, group, 1])

        @pl.when(inner)
        def _():
            arrived(state.at[s, :, part, 0], radial_recv.at[s, group, 0])

        @pl.when(outer)
        def _():
            arrived(state.at[s, :, part, height + 1], radial_recv.at[s, group, 1])

    def average(parts, ref):
        total = LAYER_WEIGHTS[0] * parts[0]
        for layer in range(1, layers):
            total = total + LAYER_WEIGHTS[layer] * parts[layer]
        mean = jnp.sum(total, axis=0, keepdims=True) / KR
        for tile in range(8):
            ref[tile : tile + 1, :] = mean[:, tile * 128 : (tile + 1) * 128]

    def start_forth(v, carry):
        for k in (2, 3, 1):
            forth(v, k).start()
        own(v).start()
        return carry

    def start_back(v, carry):
        for k in (2, 3, 1):
            back(v, k).start()
        return carry

    loads = [
        pltpu.make_async_copy(src, dst, load_sem.at[i])
        for i, (src, dst) in enumerate(((field_ref, loaded), (owner_hbm, owner_ref)))
    ]
    lax.fori_loop(0, variables, start_forth, 0)
    for load in loads:
        load.start()
    for load in loads:
        load.wait()

    @pl.when(jnp.logical_not(upper))
    def _():
        over[...] = jnp.zeros_like(over)

    @pl.when(jnp.logical_not(inner))
    def _():
        state[:, :, :, 0] = jnp.zeros((4, 2, variables, 8, 128), jnp.float32)

    @pl.when(jnp.logical_not(outer))
    def _():
        state[:, :, :, height + 1] = jnp.zeros((4, 2, variables, 8, 128), jnp.float32)

    def unweave(r, carry):
        for v in range(variables):
            for z in range(2):
                state[0, z, v, r + 1] = loaded[v, r, pl.ds(z, 8, stride=2), :]
        return carry

    lax.fori_loop(0, height, unweave, 0)

    groups = ((0, variables - late), (variables - late, variables))
    for group, (first, last) in enumerate(groups):
        def first_halo(v, carry):
            send_halo(0, v, group)
            return carry

        lax.fori_loop(first, last, first_halo, 0)

    even, half = class_counts(length)
    row = lax.broadcasted_iota(jnp.int32, (8, quarter), 0)
    target = lax.broadcasted_iota(jnp.int32, (8, quarter), 1)
    count = jnp.where(row < 2, 2 * even, jnp.where(row < 4, 2 * half, 1))
    angle = (count * (target - jnp.where(row < 6, shift_ref[0], 0))) & (length - 1)
    angle = angle.astype(jnp.float32) * (2.0 * math.pi / length)
    sines = (row == 0) | (row == 2) | (row == 5) | (row == 7)
    tab[...] = jnp.where(sines, jnp.sin(angle), jnp.cos(angle))

    def build(i, carry):
        first = pl.multiple_of(i * 128, 128)
        rows = pl.ds(first, 128)
        source = lax.broadcasted_iota(jnp.int32, (128, 4), 0) + first
        column = lax.broadcasted_iota(jnp.int32, (128, 4), 1)
        turned = (jnp.where(column < 2, 2 * even, 2 * half) * source) & (length - 1)
        turned = turned.astype(jnp.float32) * (2.0 * math.pi / length)
        cols = jnp.where((column & 1) == 0, jnp.sin(turned), jnp.cos(turned))
        values = matrix_values(length, first, 128, shift_ref[0], tab[...], cols)
        for ref, value in zip(matrices, values):
            ref[rows, :] = value
        return carry

    lax.fori_loop(0, quarter // 128, build, 0)

    def chunk(v, carry):
        own(v).wait()
        arrived(land.at[v, pl.ds(0, 3)], recv_sem.at[v])
        parts = [land[v, i].reshape(layers * block, sector) for i in range(4)]
        for i, value in enumerate(filter_quarters(parts, tab, matrices)):
            done[v, i] = value.reshape(layers, block, sector)
        store(v).start()

        @pl.when(v >= variables - late)
        def _():
            for i in range(4):
                for cell in range(owned):
                    rows = slice(cell * KR, (cell + 1) * KR)
                    average([done[v, i, layer, rows, :] for layer in range(layers)], ghost_out.at[v, i, cell])
            ghost_in[v, pl.ds(az * owned, owned)] = ghost_out[v, az]
            for k in (2, 3, 1):
                ghost_back(v, k).start()

        @pl.when(v == variables - 2)
        def _():
            start_back(0, 0)

        return carry

    lax.fori_loop(0, variables, chunk, 0)
    lax.fori_loop(1, variables, start_back, 0)

    def gather(v, group):
        @pl.when(lower)
        def _():
            ghost_down(v, group).start()

        @pl.when(inlet)
        def _():
            ghost[v, pl.ds(0, cells)] = ghost_in[v]

    def sent_ghost(v, carry):
        arrived(ghost_in.at[v, pl.ds(0, 3 * owned)], ghost_recv.at[v])
        gather(v, 1)
        return carry

    def own_ghost(v, carry):
        def local(cell, carry):
            rows = pl.ds(pl.multiple_of(cell * KR, KR), KR)
            average([out_ref[layer, v, rows, :] for layer in range(layers)], ghost_in.at[v, cell])
            return carry

        lax.fori_loop(0, cells, local, 0)
        gather(v, 0)
        return carry

    def evolve(group):
        first, last = groups[group]
        part = pl.ds(first, last - first)

        @pl.when(inlet)
        def _():
            arrived(ghost.at[part, pl.ds(cells, (axes - 1) * cells)], inlet_recv.at[group])

        for s in range(4):
            receive_halo(s, part, group)

            def stage(v, carry):
                speed = sum(jnp.where(v == i, 0.5 * value, 0.0) for i, value in enumerate(AXIAL_SPEEDS))

                def advance(r, carry):
                    here = [state[s, z, v, r + 1] for z in range(2)]
                    below = [jnp.where(inlet, ghost[v, r], under[s, v, r]), here[0]]
                    above = [here[1], over[s, v, r]]
                    for z in range(2):
                        inward, outward = state[s, z, v, r], state[s, z, v, r + 2]
                        mask = owner_ref[z, r].astype(jnp.float32)
                        rate = mask * (
                            DIFFUSION * (outward + inward + above[z] + below[z] - 4.0 * here[z])
                            - speed * (above[z] - below[z])
                            - (0.5 * SWIRL_SPEED) * (outward - inward)
                        )
                        if s == 0:
                            change[z, v, r] = rate
                        elif s < 3:
                            change[z, v, r] = change[z, v, r] + 2.0 * rate
                        start = here[z] if s == 0 else state[0, z, v, r + 1]
                        if s < 3:
                            state[s + 1, z, v, r + 1] = start + (0.5, 0.5, 1.0)[s] * rate
                        else:
                            next_ref[v, r, pl.ds(z, 8, stride=2), :] = start + (change[z, v, r] + rate) / 6.0
                    return carry

                lax.fori_loop(0, height, advance, 0, unroll=UNROLL)
                if s < 3:
                    send_halo(s + 1, v, group)
                return carry

            lax.fori_loop(first, last, stage, 0)

    lax.fori_loop(variables - late, variables, sent_ghost, 0)
    evolve(1)

    def back_arrived(v):
        arrived(out_ref.at[:, v, pl.ds(0, 3 * block)], back_recv.at[v])
        store(v).wait()

    def early(v, carry):
        back_arrived(v)
        return own_ghost(v, carry)

    lax.fori_loop(0, variables - late, early, 0)
    evolve(0)

    left(land.at[:, pl.ds(0, 3)], send_sem.at[0])
    left(ghost_out.at[pl.ds(variables - late, late), pl.ds(0, 3)], ghost_send.at[0])

    @pl.when(lower)
    def _():
        left(ghost_in, down_send.at[0])
        left(over, axial_send.at[1])

    @pl.when(upper)
    def _():
        left(under, axial_send.at[0])

    @pl.when(outer)
    def _():
        left(state.at[:, :, :, height], radial_send.at[0])

    @pl.when(inner)
    def _():
        left(state.at[:, :, :, 1], radial_send.at[1])

    for v in range(variables - late, variables):
        back_arrived(v)
    left(done.at[:, pl.ds(0, 3)], back_send.at[0])


def whole_step(cycle, field, shift, owner):
    layers, variables, radial, sector = cycle.shape
    _, height, _, _ = field.shape
    length = 4 * sector
    axes = lax.axis_size("ax")
    block = radial // 4
    owned = block // KR
    f32, bf16 = jnp.float32, jnp.bfloat16
    smem = pl.BlockSpec(memory_space=pltpu.SMEM)
    vmem = pl.BlockSpec(memory_space=pltpu.VMEM)
    hbm = pl.BlockSpec(memory_space=pl.ANY)
    dma = pltpu.SemaphoreType.DMA
    woven = (variables, height, 16, 128)
    plane = (variables, height, 8, 128)
    shifted_cycle, stepped = pl.pallas_call(
        lambda *refs: step_body(length, *refs),
        out_shape=[pltpu.VMEM(cycle.shape, f32), pltpu.VMEM(woven, f32)],
        in_specs=[smem, hbm, hbm, hbm],
        out_specs=[vmem, vmem],
        scratch_shapes=[pltpu.SMEM(owner.T.shape, jnp.int32)]
        + [pltpu.VMEM((variables, 4, layers, block, sector), f32)] * 2
        + [pltpu.VMEM((sector, sector), bf16)] * 4
        + [
            pltpu.VMEM((8, sector), f32),
            pltpu.VMEM(woven, f32),
            pltpu.VMEM((4, 2, variables, height + 2, 8, 128), f32),
            pltpu.VMEM((4,) + plane, f32),
            pltpu.VMEM((4,) + plane, f32),
            pltpu.VMEM(plane, f32),
            pltpu.VMEM((variables, 4 * owned, 8, 128), f32),
            pltpu.VMEM((variables, 4, owned, 8, 128), f32),
            pltpu.VMEM((2,) + plane, f32),
        ]
        + [dma((1,)), dma((variables,))] * 2
        + [dma((variables,)), dma((variables,)), dma((2,))]
        + [dma((1,)), dma((variables,)), dma((1,)), dma((2,))]
        + [dma((2,)), dma((4, 2, 2))] * 2,
        compiler_params=pltpu.CompilerParams(vmem_limit_bytes=44 * MIB, collective_id=0, has_side_effects=True),
        cost_estimate=pl.CostEstimate(
            flops=24 * layers * variables * radial * sector * sector,
            bytes_accessed=8 * layers * variables * radial * sector,
            transcendentals=0,
        ),
        name="whole_step",
    )(
        shift,
        pltpu.with_memory_space_constraint(owner.T, pltpu.HBM),
        cycle,
        pltpu.with_memory_space_constraint(
            field.reshape(variables, height, 2, 8, 128).transpose(0, 1, 3, 2, 4).reshape(woven), pltpu.HBM
        ),
    )
    shifted_cycle, stepped = written(shifted_cycle, stepped)
    field_next = stepped.reshape(variables, height, 8, 2, 128).transpose(0, 1, 3, 2, 4).reshape(field.shape)
    return field_next, shifted_cycle


def shifted(array, axis, dim, width):
    devices, length = (lax.axis_size(axis), array.shape[dim])
    up = [(i, (i + 1) % devices) for i in range(devices - 1)]
    down = [(j, i) for i, j in up]
    last = lax.slice_in_dim(array, length - width, length, axis=dim)
    leading = lax.slice_in_dim(array, 0, width, axis=dim)
    return lax.ppermute(last, axis, up), lax.ppermute(leading, axis, down)


def chunked(cycle, shift):
    layers, variables, radial, sector = cycle.shape
    sectors = lax.axis_size("az")
    length = sectors * sector
    shift_value = shift[0]
    tables = shift_tables(shift_value, length)
    matrices = filter_matrices(shift, tables, length)

    def across(part):
        return lax.all_to_all(part, "az", split_axis=0, concat_axis=0, tiled=True)

    def passed(pieces):
        return to_sectors(filtered(to_quarters(pieces), tables, matrices), sectors)

    lead = cycle[:1].reshape(sectors, -1, sector)
    rest = cycle[1:].reshape(sectors, -1, sector)
    lead = across(lead)

    weights = jnp.array(LAYER_WEIGHTS, jnp.float32)
    cells = radial // KR
    grouped = cycle.reshape(layers, variables, cells, KR, sector)
    mean = jnp.sum(jnp.sum(grouped * weights[:, None, None, None, None], axis=0), axis=2) / KR
    around = lax.all_gather(mean.reshape(variables * cells, sector), "az", axis=0, tiled=False)
    lead, around, rest = lax.optimization_barrier((lead, around, rest))
    rest = across(rest)

    ghost = lax.dynamic_index_in_dim(passed(around), lax.axis_index("az"), 0, keepdims=False)

    lead, rest = lax.optimization_barrier((passed(lead), rest))
    lead = across(lead).reshape(1, variables, radial, sector)
    rest = across(passed(rest)).reshape(layers - 1, variables, radial, sector)
    shifted_cycle = jnp.concatenate([lead, rest], axis=0)
    return ghost, shifted_cycle


def write_body(cycle_ref, field_ref, cycle_out, field_out, sems):
    layers = cycle_ref.shape[0]
    copies = [pltpu.make_async_copy(cycle_ref.at[i], cycle_out.at[i], sems.at[i]) for i in range(layers)]
    copies.append(pltpu.make_async_copy(field_ref, field_out, sems.at[layers]))
    for copy in copies:
        copy.start()
    for copy in copies:
        copy.wait()


def written(cycle, field):
    vmem = pl.BlockSpec(memory_space=pltpu.VMEM)
    hbm = pl.BlockSpec(memory_space=pltpu.HBM)
    return pl.pallas_call(
        write_body,
        out_shape=[pltpu.HBM(cycle.shape, cycle.dtype), pltpu.HBM(field.shape, field.dtype)],
        in_specs=[vmem, vmem],
        out_specs=[hbm, hbm],
        scratch_shapes=[pltpu.SemaphoreType.DMA((cycle.shape[0] + 1,))],
        compiler_params=pltpu.CompilerParams(vmem_limit_bytes=4 * MIB),
        name="write_results",
    )(cycle, field)


def on_device(cycle, field, shift, owner):
    layers, variables, radial, sector = cycle.shape
    sectors = lax.axis_size("az")
    if sectors == 4 and sector == 1024 and field.shape[2] == 2 and radial % (4 * KR) == 0:
        return whole_step(cycle, field, shift, owner)
    ghost, shifted_cycle = chunked(cycle, shift)
    ghost = lax.all_gather(ghost.reshape(variables, radial // KR, sector), "ax", axis=1, tiled=True)

    mask = owner.astype(jnp.float32)[None, :, :, None]
    speeds = jnp.array(AXIAL_SPEEDS, jnp.float32)[:, None, None, None]
    at_inlet = lax.axis_index("ax") == 0

    def rates(state):
        inner, outer = shifted(state, "rad", 1, 1)
        under, over = shifted(state, "ax", 2, 1)
        lower = jnp.where(at_inlet, ghost[:, :, None], under)
        outward = jnp.concatenate([state[:, 1:], outer], axis=1)
        inward = jnp.concatenate([inner, state[:, :-1]], axis=1)
        above = jnp.concatenate([state[:, :, 1:], over], axis=2)
        below = jnp.concatenate([lower, state[:, :, :-1]], axis=2)
        return mask * (
            DIFFUSION * (outward + inward + above + below - 4.0 * state)
            - 0.5 * speeds * (above - below)
            - 0.5 * SWIRL_SPEED * (outward - inward)
        )

    first = rates(field)
    second = rates(field + 0.5 * first)
    third = rates(field + 0.5 * second)
    fourth = rates(field + third)
    field_next = field + (first + 2.0 * second + 2.0 * third + fourth) / 6.0
    return (field_next, shifted_cycle)


def solution(mesh):
    in_specs = (P(None, None, ("rad", "ax"), "az"), P(None, "rad", "ax", "az"), P(), P("rad", "ax"))
    out_specs = (P(None, "rad", "ax", "az"), P(None, None, ("rad", "ax"), "az"))
    return jax.shard_map(
        on_device, mesh=mesh, in_specs=in_specs, out_specs=out_specs, check_vma=False
    )
```

```python
import math

import jax
import jax.numpy as jnp
import numpy as np
from jax import lax
from jax.experimental import pallas as pl
from jax.experimental.pallas import tpu as pltpu
from jax.sharding import PartitionSpec as P

KR = 8
LATE = 2
UNROLL = 8


LAYER_WEIGHTS = (0.4, 0.3, 0.2, 0.1)
AXIAL_SPEEDS = (0.35, 0.2, 0.3, 0.25, 0.4)
DIFFUSION = 0.15
SWIRL_SPEED = 0.1
MIB = 1024 * 1024


def class_counts(length):
    top = (length - 1) // 3
    kept = np.arange(-top, top + 1)
    first = kept[kept % 4 == 1]
    assert length % 4 == 0 and (first - 1).sum() == 0
    even, odd, half = [int((kept % 4 == r).sum()) for r in (0, 1, 2)]
    assert even == odd
    return even, half


def shift_tables(shift_value, length):
    quarter = length // 4
    even, half = class_counts(length)
    target = jnp.arange(quarter, dtype=jnp.int32) - shift_value
    rows = []
    for count in (even, half):
        angle = jnp.remainder(count * target, 2 * quarter).astype(jnp.float32) * (math.pi / quarter)
        rows += [jnp.sin(angle), jnp.cos(angle)]
    angle = jnp.remainder(target, length).astype(jnp.float32) * (2.0 * math.pi / length)
    rows += [jnp.cos(angle), jnp.sin(angle)]
    source = np.arange(quarter) * (2.0 * np.pi / length)
    rows += [jnp.asarray(np.cos(source), jnp.float32), jnp.asarray(np.sin(source), jnp.float32)]
    return jnp.stack(rows)


def source_tables(length):
    quarter = length // 4
    source = np.arange(quarter)
    cols = []
    for count in class_counts(length):
        angle = (count * source % (2 * quarter)) * (np.pi / quarter)
        cols += [np.sin(angle), np.cos(angle)]
    return jnp.asarray(np.stack(cols, axis=1), jnp.float32)


def matrix_values(length, first, block, shift_value, rows, cols):
    quarter = length // 4
    even, half = class_counts(length)
    shape = (block, quarter)
    source = lax.broadcasted_iota(jnp.int32, shape, 0) + first
    target = lax.broadcasted_iota(jnp.int32, shape, 1)
    apart = (target - source - shift_value) & (2 * quarter - 1)
    apart = jnp.where(apart >= quarter, apart - 2 * quarter, apart)
    near = jnp.where(apart > quarter // 2, quarter - apart, apart)
    near = jnp.where(apart < -(quarter // 2), -quarter - apart, near)
    u = near.astype(jnp.float32) * (math.pi / quarter)
    w = u * u
    poly = jnp.full(shape, 1.0 / 6227020800.0, jnp.float32)
    for c in (-1.0 / 39916800.0, 1.0 / 362880.0, -1.0 / 5040.0, 1.0 / 120.0, -1.0 / 6.0):
        poly = poly * w + c
    sine = u + u * (w * poly)
    zero = near == 0
    inverse = 0.25 / (quarter * jnp.where(zero, 1.0, sine))
    top_even = rows[0:1, :] * cols[:, 1:2] - rows[1:2, :] * cols[:, 0:1]
    top_half = rows[2:3, :] * cols[:, 3:4] - rows[3:4, :] * cols[:, 2:3]
    sign = jnp.where(apart == 0, 1.0, -1.0)
    m_even = jnp.where(zero, 0.25 * even / quarter, top_even * inverse)
    m_half = jnp.where(zero, sign * (0.25 * half / quarter), top_half * inverse)
    return split(m_even) + split(m_half)


def kernel_matrix_body(length, block, shift_ref, rows_ref, cols_ref, *out_refs):
    first = pl.program_id(0) * block
    values = matrix_values(length, first, block, shift_ref[0], rows_ref[...], cols_ref[...])
    for ref, value in zip(out_refs, values):
        ref[...] = value


def filter_matrices(shift, tables, length):
    quarter = length // 4
    block = 128
    out = jax.ShapeDtypeStruct((quarter, quarter), jnp.bfloat16)
    return pl.pallas_call(
        lambda *refs: kernel_matrix_body(length, block, *refs),
        grid=(quarter // block,),
        out_shape=[out] * 4,
        in_specs=[
            pl.BlockSpec(memory_space=pltpu.SMEM),
            pl.BlockSpec((8, quarter), lambda i: (0, 0)),
            pl.BlockSpec((block, 4), lambda i: (i, 0)),
        ],
        out_specs=[pl.BlockSpec((block, quarter), lambda i: (i, 0))] * 4,
        compiler_params=pltpu.CompilerParams(vmem_limit_bytes=32 * MIB),
        cost_estimate=pl.CostEstimate(flops=60 * quarter * quarter, bytes_accessed=8 * quarter * quarter, transcendentals=0),
        name="filter_matrices",
    )(shift, tables, source_tables(length))


def split(value):
    high = value.astype(jnp.bfloat16)
    return high, (value - high.astype(jnp.float32)).astype(jnp.bfloat16)


def product(value, high_ref, low_ref):
    high, low = split(value)
    f32 = jnp.float32
    return (
        jnp.dot(high, low_ref[...], preferred_element_type=f32)
        + jnp.dot(low, high_ref[...], preferred_element_type=f32)
        + jnp.dot(high, high_ref[...], preferred_element_type=f32)
    )


def filter_quarters(parts, tab_ref, matrix_refs):
    x0, x1, x2, x3 = parts
    count = x0.shape[0]
    eh_ref, el_ref, hh_ref, hl_ref = matrix_refs
    cos_t, sin_t = 2.0 * tab_ref[4:5, :], 2.0 * tab_ref[5:6, :]
    cos_s, sin_s = tab_ref[6:7, :], tab_ref[7:8, :]
    even, odd = x0 + x2, x1 + x3
    re, im = x0 - x2, x3 - x1
    stacked = jnp.concatenate([even + odd, re * cos_s + im * sin_s, im * cos_s - re * sin_s], axis=0)
    turned = product(stacked, eh_ref, el_ref)
    z2 = product(even - odd, hh_ref, hl_ref)
    z0, ure, uim = turned[:count], turned[count : 2 * count], turned[2 * count :]
    zre = cos_t * ure - sin_t * uim
    zim = cos_t * uim + sin_t * ure
    plus, minus = z0 + z2, z0 - z2
    return plus + zre, minus - zim, plus - zre, minus + zim


def filter_body(x_ref, tab_ref, eh_ref, el_ref, hh_ref, hl_ref, out_ref):
    values = filter_quarters([x_ref[i] for i in range(4)], tab_ref, (eh_ref, el_ref, hh_ref, hl_ref))
    for i, value in enumerate(values):
        out_ref[i] = value


def filtered(quarters, tables, matrices):
    _, count, quarter = quarters.shape
    block = next((b for b in (80, 64, 40, 32, 16, 8) if count % b == 0), count)
    whole = pl.BlockSpec((quarter, quarter), lambda i: (0, 0))
    part = pl.BlockSpec((4, block, quarter), lambda i: (0, i, 0))
    return pl.pallas_call(
        filter_body,
        grid=(count // block,),
        out_shape=jax.ShapeDtypeStruct(quarters.shape, jnp.float32),
        in_specs=[part, pl.BlockSpec((8, quarter), lambda i: (0, 0))] + [whole] * 4,
        out_specs=part,
        compiler_params=pltpu.CompilerParams(vmem_limit_bytes=48 * MIB),
        cost_estimate=pl.CostEstimate(
            flops=24 * count * quarter * quarter,
            bytes_accessed=32 * count * quarter + 8 * quarter * quarter,
            transcendentals=0,
        ),
        name="spectral_filter",
    )(quarters, tables, *matrices)


def to_quarters(pieces):
    sectors, count, sector = pieces.shape
    per = sectors // 4
    if per == 1:
        return pieces
    return pieces.reshape(4, per, count, sector).transpose(0, 2, 1, 3).reshape(4, count, per * sector)


def to_sectors(quarters, sectors):
    _, count, quarter = quarters.shape
    per = sectors // 4
    if per == 1:
        return quarters
    sector = quarter // per
    return quarters.reshape(4, count, per, sector).transpose(0, 2, 1, 3).reshape(sectors, count, sector)


def step_body(length, shift_ref, owner_hbm, cycle_ref, field_ref, out_ref, next_ref,
              owner_ref, land, done, eh, el, hh, hl, tab, loaded, state, under, over, ghost, ghost_in, ghost_out, change,
              send_sem, recv_sem, back_send, back_recv, own_sem, store_sem, load_sem,
              ghost_send, ghost_recv, down_send, inlet_recv, axial_send, axial_recv, radial_send, radial_recv):
    layers, variables, radial, sector = cycle_ref.shape
    quarter = length // 4
    block = radial // 4
    owned = block // KR
    cells = radial // KR
    height = next_ref.shape[1]
    az, rad, ax = lax.axis_index("az"), lax.axis_index("rad"), lax.axis_index("ax")
    rads, axes = lax.axis_size("rad"), lax.axis_size("ax")
    inner, outer = rad > 0, rad < rads - 1
    inlet, lower, upper = ax == 0, ax > 0, ax < axes - 1
    late = min(LATE, variables)
    matrices = (eh, el, hh, hl)
    mesh_id = pl.DeviceIdType.MESH

    barrier = pltpu.get_barrier_semaphore()
    for peer in [{"az": lax.rem(az + i, 4)} for i in (1, 2, 3)] + [{"ax": lax.rem(ax + j, axes)} for j in range(1, axes)]:
        pl.semaphore_signal(barrier, inc=1, device_id=peer, device_id_type=mesh_id)

    @pl.when(inner)
    def _():
        pl.semaphore_signal(barrier, inc=1, device_id={"rad": rad - 1}, device_id_type=mesh_id)

    @pl.when(outer)
    def _():
        pl.semaphore_signal(barrier, inc=1, device_id={"rad": rad + 1}, device_id_type=mesh_id)

    pl.semaphore_wait(barrier, axes + 2 + inner.astype(jnp.int32) + outer.astype(jnp.int32))

    def partner(k):
        return (None, az + 1 - 2 * lax.rem(az, 2), lax.rem(az + 2, 4), 3 - az)[k]

    def rows_of(index):
        return pl.ds(pl.multiple_of(index * block, block), block)

    def remote(src, dst, send, recv, peer):
        return pltpu.make_async_remote_copy(
            src_ref=src, dst_ref=dst, send_sem=send, recv_sem=recv, device_id=peer, device_id_type=mesh_id
        )

    def forth(v, k):
        peer = partner(k)
        return remote(
            cycle_ref.at[:, v, rows_of(peer)], land.at[v, az], send_sem.at[0], recv_sem.at[v], {"az": peer}
        )

    def back(v, k):
        peer = partner(k)
        return remote(
            done.at[v, peer], out_ref.at[:, v, rows_of(az)], back_send.at[0], back_recv.at[v], {"az": peer}
        )

    def own(v):
        return pltpu.make_async_copy(cycle_ref.at[:, v, rows_of(az)], land.at[v, az], own_sem.at[v])

    def store(v):
        return pltpu.make_async_copy(done.at[v, az], out_ref.at[:, v, rows_of(az)], store_sem.at[v])

    def arrived(ref, semaphore):
        remote(ref, ref, semaphore, semaphore, {"az": partner(1)}).wait_recv()

    def left(ref, semaphore):
        remote(ref, ref, semaphore, semaphore, {"az": partner(1)}).wait_send()

    def ghost_back(v, k):
        peer = partner(k)
        return remote(
            ghost_out.at[v, peer], ghost_in.at[v, pl.ds(az * owned, owned)], ghost_send.at[0], ghost_recv.at[v], {"az": peer}
        )

    def ghost_down(v, group):
        return remote(
            ghost_in.at[v], ghost.at[v, pl.ds(ax * cells, cells)], down_send.at[0], inlet_recv.at[group], {"ax": 0}
        )

    def send_halo(s, v, group):
        @pl.when(upper)
        def _():
            remote(
                state.at[s, 1, v, pl.ds(1, height)], under.at[s, v], axial_send.at[0], axial_recv.at[s, group, 0], {"ax": ax + 1}
            ).start()

        @pl.when(lower)
        def _():
            remote(
                state.at[s, 0, v, pl.ds(1, height)], over.at[s, v], axial_send.at[1], axial_recv.at[s, group, 1], {"ax": ax - 1}
            ).start()

        @pl.when(outer)
        def _():
            remote(
                state.at[s, :, v, height], state.at[s, :, v, 0], radial_send.at[0], radial_recv.at[s, group, 0], {"rad": rad + 1}
            ).start()

        @pl.when(inner)
        def _():
            remote(
                state.at[s, :, v, 1], state.at[s, :, v, height + 1], radial_send.at[1], radial_recv.at[s, group, 1], {"rad": rad - 1}
            ).start()

    def receive_halo(s, part, group):
        @pl.when(lower)
        def _():
            arrived(under.at[s, part], axial_recv.at[s, group, 0])

        @pl.when(upper)
        def _():
            arrived(over.at[s, part], axial_recv.at[s, group, 1])

        @pl.when(inner)
        def _():
            arrived(state.at[s, :, part, 0], radial_recv.at[s, group, 0])

        @pl.when(outer)
        def _():
            arrived(state.at[s, :, part, height + 1], radial_recv.at[s, group, 1])

    def average(parts, ref):
        total = LAYER_WEIGHTS[0] * parts[0]
        for layer in range(1, layers):
            total = total + LAYER_WEIGHTS[layer] * parts[layer]
        mean = jnp.sum(total, axis=0, keepdims=True) / KR
        for tile in range(8):
            ref[tile : tile + 1, :] = mean[:, tile * 128 : (tile + 1) * 128]

    def start_forth(v, carry):
        for k in (2, 3, 1):
            forth(v, k).start()
        own(v).start()
        return carry

    def start_back(v, carry):
        for k in (2, 3, 1):
            back(v, k).start()
        return carry

    loads = [
        pltpu.make_async_copy(src, dst, load_sem.at[i])
        for i, (src, dst) in enumerate(((field_ref, loaded), (owner_hbm, owner_ref)))
    ]
    lax.fori_loop(0, variables, start_forth, 0)
    for load in loads:
        load.start()
    for load in loads:
        load.wait()

    @pl.when(jnp.logical_not(upper))
    def _():
        over[...] = jnp.zeros_like(over)

    @pl.when(jnp.logical_not(inner))
    def _():
        state[:, :, :, 0] = jnp.zeros((4, 2, variables, 8, 128), jnp.float32)

    @pl.when(jnp.logical_not(outer))
    def _():
        state[:, :, :, height + 1] = jnp.zeros((4, 2, variables, 8, 128), jnp.float32)

    def unweave(r, carry):
        for v in range(variables):
            for z in range(2):
                state[0, z, v, r + 1] = loaded[v, r, pl.ds(z, 8, stride=2), :]
        return carry

    lax.fori_loop(0, height, unweave, 0)

    groups = ((0, variables - late), (variables - late, variables))
    for group, (first, last) in enumerate(groups):
        def first_halo(v, carry):
            send_halo(0, v, group)
            return carry

        lax.fori_loop(first, last, first_halo, 0)

    even, half = class_counts(length)
    row = lax.broadcasted_iota(jnp.int32, (8, quarter), 0)
    target = lax.broadcasted_iota(jnp.int32, (8, quarter), 1)
    count = jnp.where(row < 2, 2 * even, jnp.where(row < 4, 2 * half, 1))
    angle = (count * (target - jnp.where(row < 6, shift_ref[0], 0))) & (length - 1)
    angle = angle.astype(jnp.float32) * (2.0 * math.pi / length)
    sines = (row == 0) | (row == 2) | (row == 5) | (row == 7)
    tab[...] = jnp.where(sines, jnp.sin(angle), jnp.cos(angle))

    def build(i, carry):
        first = pl.multiple_of(i * 128, 128)
        rows = pl.ds(first, 128)
        source = lax.broadcasted_iota(jnp.int32, (128, 4), 0) + first
        column = lax.broadcasted_iota(jnp.int32, (128, 4), 1)
        turned = (jnp.where(column < 2, 2 * even, 2 * half) * source) & (length - 1)
        turned = turned.astype(jnp.float32) * (2.0 * math.pi / length)
        cols = jnp.where((column & 1) == 0, jnp.sin(turned), jnp.cos(turned))
        values = matrix_values(length, first, 128, shift_ref[0], tab[...], cols)
        for ref, value in zip(matrices, values):
            ref[rows, :] = value
        return carry

    lax.fori_loop(0, quarter // 128, build, 0)

    def chunk(v, carry):
        own(v).wait()
        arrived(land.at[v, pl.ds(0, 3)], recv_sem.at[v])
        parts = [land[v, i].reshape(layers * block, sector) for i in range(4)]
        for i, value in enumerate(filter_quarters(parts, tab, matrices)):
            done[v, i] = value.reshape(layers, block, sector)
        store(v).start()

        @pl.when(v >= variables - late)
        def _():
            for i in range(4):
                for cell in range(owned):
                    rows = slice(cell * KR, (cell + 1) * KR)
                    average([done[v, i, layer, rows, :] for layer in range(layers)], ghost_out.at[v, i, cell])
            ghost_in[v, pl.ds(az * owned, owned)] = ghost_out[v, az]
            for k in (2, 3, 1):
                ghost_back(v, k).start()

        @pl.when(v == variables - 2)
        def _():
            start_back(0, 0)

        return carry

    lax.fori_loop(0, variables, chunk, 0)
    lax.fori_loop(1, variables, start_back, 0)

    def gather(v, group):
        @pl.when(lower)
        def _():
            ghost_down(v, group).start()

        @pl.when(inlet)
        def _():
            ghost[v, pl.ds(0, cells)] = ghost_in[v]

    def sent_ghost(v, carry):
        arrived(ghost_in.at[v, pl.ds(0, 3 * owned)], ghost_recv.at[v])
        gather(v, 1)
        return carry

    def own_ghost(v, carry):
        def local(cell, carry):
            rows = pl.ds(pl.multiple_of(cell * KR, KR), KR)
            average([out_ref[layer, v, rows, :] for layer in range(layers)], ghost_in.at[v, cell])
            return carry

        lax.fori_loop(0, cells, local, 0)
        gather(v, 0)
        return carry

    def evolve(group):
        first, last = groups[group]
        part = pl.ds(first, last - first)

        @pl.when(inlet)
        def _():
            arrived(ghost.at[part, pl.ds(cells, (axes - 1) * cells)], inlet_recv.at[group])

        for s in range(4):
            receive_halo(s, part, group)

            def stage(v, carry):
                speed = sum(jnp.where(v == i, 0.5 * value, 0.0) for i, value in enumerate(AXIAL_SPEEDS))

                def advance(r, carry):
                    here = [state[s, z, v, r + 1] for z in range(2)]
                    below = [jnp.where(inlet, ghost[v, r], under[s, v, r]), here[0]]
                    above = [here[1], over[s, v, r]]
                    for z in range(2):
                        inward, outward = state[s, z, v, r], state[s, z, v, r + 2]
                        mask = owner_ref[z, r].astype(jnp.float32)
                        rate = mask * (
                            DIFFUSION * (outward + inward + above[z] + below[z] - 4.0 * here[z])
                            - speed * (above[z] - below[z])
                            - (0.5 * SWIRL_SPEED) * (outward - inward)
                        )
                        if s == 0:
                            change[z, v, r] = rate
                        elif s < 3:
                            change[z, v, r] = change[z, v, r] + 2.0 * rate
                        start = here[z] if s == 0 else state[0, z, v, r + 1]
                        if s < 3:
                            state[s + 1, z, v, r + 1] = start + (0.5, 0.5, 1.0)[s] * rate
                        else:
                            next_ref[v, r, pl.ds(z, 8, stride=2), :] = start + (change[z, v, r] + rate) / 6.0
                    return carry

                lax.fori_loop(0, height, advance, 0, unroll=UNROLL)
                if s < 3:
                    send_halo(s + 1, v, group)
                return carry

            lax.fori_loop(first, last, stage, 0)

    lax.fori_loop(variables - late, variables, sent_ghost, 0)
    evolve(1)

    def back_arrived(v):
        arrived(out_ref.at[:, v, pl.ds(0, 3 * block)], back_recv.at[v])
        store(v).wait()

    def early(v, carry):
        back_arrived(v)
        return own_ghost(v, carry)

    lax.fori_loop(0, variables - late, early, 0)
    evolve(0)

    left(land.at[:, pl.ds(0, 3)], send_sem.at[0])
    left(ghost_out.at[pl.ds(variables - late, late), pl.ds(0, 3)], ghost_send.at[0])

    @pl.when(lower)
    def _():
        left(ghost_in, down_send.at[0])
        left(over, axial_send.at[1])

    @pl.when(upper)
    def _():
        left(under, axial_send.at[0])

    @pl.when(outer)
    def _():
        left(state.at[:, :, :, height], radial_send.at[0])

    @pl.when(inner)
    def _():
        left(state.at[:, :, :, 1], radial_send.at[1])

    for v in range(variables - late, variables):
        back_arrived(v)
    left(done.at[:, pl.ds(0, 3)], back_send.at[0])


def whole_step(cycle, field, shift, owner):
    layers, variables, radial, sector = cycle.shape
    _, height, _, _ = field.shape
    length = 4 * sector
    axes = lax.axis_size("ax")
    block = radial // 4
    owned = block // KR
    f32, bf16 = jnp.float32, jnp.bfloat16
    smem = pl.BlockSpec(memory_space=pltpu.SMEM)
    vmem = pl.BlockSpec(memory_space=pltpu.VMEM)
    hbm = pl.BlockSpec(memory_space=pl.ANY)
    dma = pltpu.SemaphoreType.DMA
    woven = (variables, height, 16, 128)
    plane = (variables, height, 8, 128)
    shifted_cycle, stepped = pl.pallas_call(
        lambda *refs: step_body(length, *refs),
        out_shape=[pltpu.VMEM(cycle.shape, f32), pltpu.VMEM(woven, f32)],
        in_specs=[smem, hbm, hbm, hbm],
        out_specs=[vmem, vmem],
        scratch_shapes=[pltpu.SMEM(owner.T.shape, jnp.int32)]
        + [pltpu.VMEM((variables, 4, layers, block, sector), f32)] * 2
        + [pltpu.VMEM((sector, sector), bf16)] * 4
        + [
            pltpu.VMEM((8, sector), f32),
            pltpu.VMEM(woven, f32),
            pltpu.VMEM((4, 2, variables, height + 2, 8, 128), f32),
            pltpu.VMEM((4,) + plane, f32),
            pltpu.VMEM((4,) + plane, f32),
            pltpu.VMEM(plane, f32),
            pltpu.VMEM((variables, 4 * owned, 8, 128), f32),
            pltpu.VMEM((variables, 4, owned, 8, 128), f32),
            pltpu.VMEM((2,) + plane, f32),
        ]
        + [dma((1,)), dma((variables,))] * 2
        + [dma((variables,)), dma((variables,)), dma((2,))]
        + [dma((1,)), dma((variables,)), dma((1,)), dma((2,))]
        + [dma((2,)), dma((4, 2, 2))] * 2,
        compiler_params=pltpu.CompilerParams(vmem_limit_bytes=44 * MIB, collective_id=0, has_side_effects=True),
        cost_estimate=pl.CostEstimate(
            flops=24 * layers * variables * radial * sector * sector,
            bytes_accessed=8 * layers * variables * radial * sector,
            transcendentals=0,
        ),
        name="whole_step",
    )(
        shift,
        pltpu.with_memory_space_constraint(owner.T, pltpu.HBM),
        cycle,
        pltpu.with_memory_space_constraint(
            field.reshape(variables, height, 2, 8, 128).transpose(0, 1, 3, 2, 4).reshape(woven), pltpu.HBM
        ),
    )
    shifted_cycle, stepped = written(shifted_cycle, stepped)
    field_next = stepped.reshape(variables, height, 8, 2, 128).transpose(0, 1, 3, 2, 4).reshape(field.shape)
    return field_next, shifted_cycle


def shifted(array, axis, dim, width):
    devices, length = (lax.axis_size(axis), array.shape[dim])
    up = [(i, (i + 1) % devices) for i in range(devices - 1)]
    down = [(j, i) for i, j in up]
    last = lax.slice_in_dim(array, length - width, length, axis=dim)
    leading = lax.slice_in_dim(array, 0, width, axis=dim)
    return lax.ppermute(last, axis, up), lax.ppermute(leading, axis, down)


def chunked(cycle, shift):
    layers, variables, radial, sector = cycle.shape
    sectors = lax.axis_size("az")
    length = sectors * sector
    shift_value = shift[0]
    tables = shift_tables(shift_value, length)
    matrices = filter_matrices(shift, tables, length)

    def across(part):
        return lax.all_to_all(part, "az", split_axis=0, concat_axis=0, tiled=True)

    def passed(pieces):
        return to_sectors(filtered(to_quarters(pieces), tables, matrices), sectors)

    lead = cycle[:1].reshape(sectors, -1, sector)
    rest = cycle[1:].reshape(sectors, -1, sector)
    lead = across(lead)

    weights = jnp.array(LAYER_WEIGHTS, jnp.float32)
    cells = radial // KR
    grouped = cycle.reshape(layers, variables, cells, KR, sector)
    mean = jnp.sum(jnp.sum(grouped * weights[:, None, None, None, None], axis=0), axis=2) / KR
    around = lax.all_gather(mean.reshape(variables * cells, sector), "az", axis=0, tiled=False)
    lead, around, rest = lax.optimization_barrier((lead, around, rest))
    rest = across(rest)

    ghost = lax.dynamic_index_in_dim(passed(around), lax.axis_index("az"), 0, keepdims=False)

    lead, rest = lax.optimization_barrier((passed(lead), rest))
    lead = across(lead).reshape(1, variables, radial, sector)
    rest = across(passed(rest)).reshape(layers - 1, variables, radial, sector)
    shifted_cycle = jnp.concatenate([lead, rest], axis=0)
    return ghost, shifted_cycle


def write_body(cycle_ref, field_ref, cycle_out, field_out, sems):
    layers = cycle_ref.shape[0]
    copies = [pltpu.make_async_copy(cycle_ref.at[i], cycle_out.at[i], sems.at[i]) for i in range(layers)]
    copies.append(pltpu.make_async_copy(field_ref, field_out, sems.at[layers]))
    for copy in copies:
        copy.start()
    for copy in copies:
        copy.wait()


def written(cycle, field):
    vmem = pl.BlockSpec(memory_space=pltpu.VMEM)
    hbm = pl.BlockSpec(memory_space=pltpu.HBM)
    return pl.pallas_call(
        write_body,
        out_shape=[pltpu.HBM(cycle.shape, cycle.dtype), pltpu.HBM(field.shape, field.dtype)],
        in_specs=[vmem, vmem],
        out_specs=[hbm, hbm],
        scratch_shapes=[pltpu.SemaphoreType.DMA((cycle.shape[0] + 1,))],
        compiler_params=pltpu.CompilerParams(vmem_limit_bytes=4 * MIB),
        name="write_results",
    )(cycle, field)


def on_device(cycle, field, shift, owner):
    layers, variables, radial, sector = cycle.shape
    sectors = lax.axis_size("az")
    if sectors == 4 and sector == 1024 and field.shape[2] == 2 and radial % (4 * KR) == 0:
        return whole_step(cycle, field, shift, owner)
    ghost, shifted_cycle = chunked(cycle, shift)
    ghost = lax.all_gather(ghost.reshape(variables, radial // KR, sector), "ax", axis=1, tiled=True)

    mask = owner.astype(jnp.float32)[None, :, :, None]
    speeds = jnp.array(AXIAL_SPEEDS, jnp.float32)[:, None, None, None]
    at_inlet = lax.axis_index("ax") == 0

    def rates(state):
        inner, outer = shifted(state, "rad", 1, 1)
        under, over = shifted(state, "ax", 2, 1)
        lower = jnp.where(at_inlet, ghost[:, :, None], under)
        outward = jnp.concatenate([state[:, 1:], outer], axis=1)
        inward = jnp.concatenate([inner, state[:, :-1]], axis=1)
        above = jnp.concatenate([state[:, :, 1:], over], axis=2)
        below = jnp.concatenate([lower, state[:, :, :-1]], axis=2)
        return mask * (
            DIFFUSION * (outward + inward + above + below - 4.0 * state)
            - 0.5 * speeds * (above - below)
            - 0.5 * SWIRL_SPEED * (outward - inward)
        )

    first = rates(field)
    second = rates(field + 0.5 * first)
    third = rates(field + 0.5 * second)
    fourth = rates(field + third)
    field_next = field + (first + 2.0 * second + 2.0 * third + fourth) / 6.0
    return (field_next, shifted_cycle)


def solution(mesh):
    in_specs = (P(None, None, ("rad", "ax"), "az"), P(None, "rad", "ax", "az"), P(), P("rad", "ax"))
    out_specs = (P(None, "rad", "ax", "az"), P(None, None, ("rad", "ax"), "az"))
    return jax.shard_map(
        on_device, mesh=mesh, in_specs=in_specs, out_specs=out_specs, check_vma=False
    )
```
